256 devices in a mesh: cells: 64 (over x_lo, y, z), tracers: 4 (over x_hi, core).
Axes of the slice: x: 4 (x_hi: 2, x_lo: 2; x = x_hi * 2 + x_lo), y: 4, z: 8, core: 2. Of those that a mesh axis runs over, the one named last changes fastest.
Arguments:
- pulses: float32 [4096, 256, 128], P('tracers', 'cells'), may hold values from -6 to 6
- wind_x: float32 [256, 128], P('cells'), may hold values from -0.24 to 0.24
- wind_y: float32 [256, 128], P('cells'), may hold values from -0.24 to 0.24
- obs_tile: int32 [8192, 1], P('cells'), may hold values from 0 to 63; in each aligned block of 128 rows (0 to 127, 128 to 255, ...) at most 4 rows name the same one
- obs_weight: bfloat16 [8192, 512], P('cells'), may hold values from 0.099609375 to 10
- obs_precision: bfloat16 [8192], P('cells'), may hold values from 0.0029907227 to 0.099609375
Outputs:
- gram: float32 [4096, 4096], P('cells', 'tracers')
The draws below stay inside these ranges and needn't reach their ends.
Inputs may be any that keep to these rules, and one draw needn't show every extreme that they name: `obs_tile`: among the rows of one index of cells no tile is named by more than 4 rows, a bound that some block reaches of them.
All inputs are finite; a program needn't handle non-finite values.
Results may differ from the reference program's by a relative error of at most 0.0031.
Values may be sent and summed in bfloat16 or wider, within the bound.
No kernel may reach another device: no remote copies, remote signals or barrier semaphores. Data moves between devices by JAX's collectives and lax.ppermute only.
A program may use at most 64 MiB of HBM per device.

```python
import math
import jax
import jax.numpy as jnp
import numpy as np
from jax import lax

K = 4096
ROWS_DEV = 4
COLS = 128
STEPS = 3
OBS_DEV = 128
ROWS = 256
TILE = 512
OBS = 8192
CAP = 4
N_CELLS = 64


def shard_levels(key, extent, cuts, smallest, largest):
    factor_of = 1.0
    for position, blocks in cuts:
        steps = jax.random.uniform(jax.random.fold_in(jax.random.fold_in(key, 6), position), (blocks,), jnp.float32, smallest / len(cuts), largest / len(cuts))
        factor_of = factor_of * jnp.repeat(jnp.exp(steps), extent[position] // blocks).reshape((-1,) + (1,) * (len(extent) - 1 - position))
    return factor_of


def shared_out(rng, own, number, rows, amount, top, bound, skew):
    order = jax.random.permutation(rng, amount)
    packed, usual = portions_of(amount, rows * top, bound, skew, True), portions_of(amount, rows * top, bound, skew, False)
    places = jnp.arange(amount)

    def named(tallies, offset_by):
        used = int((tallies > 0).sum())
        fixed = max(1, used // 4)
        moved = fixed + (places - fixed + offset_by * (used - fixed)) % max(1, amount - fixed)
        return jnp.zeros((amount,), jnp.int32).at[order[jnp.where(places < fixed, places, moved)]].set(jnp.asarray(tallies, jnp.int32))

    tallies = jnp.where(number % 4 == 0, named(packed, number // 4), named(usual, number - number // 4 - 1))
    mixed = jax.random.permutation(jax.random.fold_in(own, 3), amount)
    giver, receiver = mixed[0:amount // 2 * 2:2], mixed[1:amount // 2 * 2:2]
    margin = jnp.minimum(tallies[giver] - 1, bound - tallies[receiver]) // 2
    margin = jnp.where((giver == order[0]) | (receiver == order[0]) | (tallies[receiver] == 0), 0, jnp.maximum(margin, 0))
    moved = jax.random.randint(jax.random.fold_in(own, 4), (amount // 2,), 0, 1 << 20) % (margin + 1)
    tallies = tallies.at[giver].add(-moved).at[receiver].add(moved)
    labels = jnp.searchsorted(jnp.cumsum(tallies), jnp.arange(rows * top), side="right").astype(jnp.int32)
    listing = labels.reshape(top, rows).T
    listing = listing[jax.random.permutation(jax.random.fold_in(own, 1), rows)]
    offset_by = jax.random.randint(jax.random.fold_in(own, 2), (rows, 1), 0, top)
    return jnp.take_along_axis(listing, (jnp.arange(top)[None, :] + offset_by) % top, axis=1)


def portions_of(number_of, total, bound, skew, full):
    loads = [(1 << 20) // math.isqrt(standing ** skew) + 1 for standing in range(1, number_of + 1)]
    largest = bound if full else min(bound, max(-(-total // number_of), total * loads[0] // sum(loads)))
    least = 1 if total - largest >= number_of - 1 else 0
    holding, rest = [largest] + [least] * (number_of - 1), total - largest - least * (number_of - 1)
    while rest > 0:
        free = [i for i in range(1, number_of) if holding[i] < largest] or [i for i in range(1, number_of) if holding[i] < bound]
        whole, budget = sum([loads[i] for i in free]), rest
        for i in free:
            addition = min(bound - holding[i], max(1, budget * loads[i] // whole), rest)
            holding[i] = holding[i] + addition
            rest = rest - addition
    return np.array(holding)


def bell_draw(own_key, extent, scale, bound, cuts=(), kind=jnp.bfloat16):
    entries = jax.random.normal(own_key, extent, jnp.float32) * scale
    if len(cuts) > 0:
        entries = shard_levels(own_key, extent, cuts, -0.22, 0.18) * entries
    return jnp.clip(entries, min=-bound, max=bound).astype(kind)


def setup_inputs(seed: int = 0) -> dict:
    key_list = jax.random.split(jax.random.key(seed), 7)
    pulses = bell_draw(key_list[0], (K, ROWS, COLS), 1.0, 6.0, ((0, 4), (1, 64)), jnp.float32)
    wind_x = jnp.clip(jax.random.uniform(key_list[1], (ROWS, COLS), jnp.float32, -0.24, 0.24) * shard_levels(key_list[1], (ROWS, COLS), ((0, 64),), -0.4, 0.0), -0.24, 0.24)
    wind_y = jnp.clip(jax.random.uniform(key_list[2], (ROWS, COLS), jnp.float32, -0.24, 0.24) * shard_levels(key_list[2], (ROWS, COLS), ((0, 64),), -0.4, 0.0), -0.24, 0.24)
    obs_tile_keys = jax.random.split(jax.random.fold_in(key_list[3], 1), OBS // OBS_DEV)
    obs_tile_turns = jax.random.permutation(jax.random.fold_in(key_list[3], 3), OBS // OBS_DEV)
    obs_tile = jax.vmap(lambda own, number: shared_out(jax.random.fold_in(key_list[3], 2), own, number, OBS_DEV, N_CELLS, 1, CAP, 2))(obs_tile_keys, obs_tile_turns).reshape((OBS, 1))
    obs_weight = jnp.clip(jnp.exp(math.log(10.0) - 4.609084 * jax.random.uniform(key_list[4], (OBS, TILE), jnp.float32) ** shard_levels(key_list[4], (OBS, TILE), ((0, 64),), -0.2, 0.2)), 0.099609375, 10.0).astype(jnp.bfloat16)
    obs_precision = jnp.clip(jnp.exp(math.log(0.099609375) - 3.5057412 * jax.random.uniform(key_list[5], (OBS,), jnp.float32) ** shard_levels(key_list[5], (OBS,), ((0, 64),), -0.2, 0.2)), 0.0029907227, 0.099609375).astype(jnp.bfloat16)
    return {"pulses": pulses, "wind_x": wind_x, "wind_y": wind_y, "obs_tile": obs_tile, "obs_weight": obs_weight, "obs_precision": obs_precision}


def transport(tracer_field, wind_x, wind_y):
    for index_step in range(STEPS):
        behind = jnp.roll(tracer_field, 1, axis=2)
        flux_x = jnp.maximum(wind_x, 0.0) * behind + jnp.minimum(wind_x, 0.0) * tracer_field
        row_above = jnp.roll(tracer_field, 1, axis=1)
        flux_y = jnp.maximum(wind_y, 0.0) * row_above + jnp.minimum(wind_y, 0.0) * tracer_field
        tracer_field = tracer_field + flux_x - jnp.roll(flux_x, -1, axis=2) + flux_y - jnp.roll(flux_y, -1, axis=1)
    return tracer_field


def reference(pulses, wind_x, wind_y, obs_tile, obs_weight, obs_precision):
    blocks = pulses.reshape(K // 64, 64, ROWS, COLS)
    advected = lax.map(lambda block_one: transport(block_one, wind_x, wind_y).astype(jnp.bfloat16), blocks)
    final_field = advected.reshape(K, ROWS, COLS)
    weights_wide = obs_weight.astype(jnp.float32)
    averaging = (weights_wide / jnp.sum(weights_wide, axis=1, keepdims=True)).astype(jnp.bfloat16)
    tile_index = obs_tile[:, 0]
    slot_total = 2 * OBS_DEV
    precision_wide = obs_precision.astype(jnp.float32)

    def per_tile(carry_rows, tile_number):
        jac_all, weighted_all = carry_rows
        matches = tile_index == tile_number
        found_rows = jnp.nonzero(matches, size=slot_total, fill_value=0)[0].astype(jnp.int32)
        live_count = jnp.sum(matches.astype(jnp.int32))
        live_slot = jnp.arange(slot_total, dtype=jnp.int32) < live_count
        sampled = lax.dynamic_slice_in_dim(final_field, (tile_number * ROWS_DEV).astype(jnp.int32), ROWS_DEV, 1)
        sampled = sampled.reshape(K, ROWS_DEV * COLS)
        jac_tile = jnp.dot(averaging[found_rows], sampled.T, preferred_element_type=jnp.float32).astype(jnp.bfloat16)
        weighted_tile = (precision_wide[found_rows][:, None] * jac_tile.astype(jnp.float32)).astype(jnp.bfloat16)
        target = jnp.where(live_slot, found_rows, OBS).astype(jnp.int32)
        jac_all = jac_all.at[target].set(jac_tile, mode="drop")
        weighted_all = weighted_all.at[target].set(weighted_tile, mode="drop")
        return (jac_all, weighted_all), None

    start_rows = (jnp.zeros((OBS, K), jnp.bfloat16), jnp.zeros((OBS, K), jnp.bfloat16))
    (jac_all, weighted_all), unused = lax.scan(per_tile, start_rows, jnp.arange(N_CELLS, dtype=jnp.int32))
    return jnp.dot(jac_all.T, weighted_all, preferred_element_type=jnp.float32)
```

```python
import jax
import jax.numpy as jnp
from jax import lax
from jax.experimental import pallas as pl
from jax.experimental.pallas import tpu as pltpu
from jax.sharding import Mesh, PartitionSpec as P

STEPS = 3
CAP = 4
XY = ("xl", "y")
CELLS = ("xl", "y", "z")
TRACERS = ("xh", "core")


def shifted(value, axis, steps):
    count = lax.axis_size(axis)
    return lax.ppermute(value, axis, [(i, (i + steps) % count) for i in range(count)])


def exchanged(value, axis):
    return lax.all_to_all(value, axis, split_axis=0, concat_axis=0, tiled=True)


def edge_rows(pulse_ref, first_ref, last_ref):
    count = first_ref.shape[1]
    rows = [pulse_ref[pl.ds(r, count, 4), :].astype(jnp.bfloat16) for r in range(4)]
    for r in range(STEPS):
        first_ref[r] = rows[r]
        last_ref[r] = rows[r + 1]


def edges(pulses, block=256):
    tracers = pulses.shape[0] // 4
    half = pl.BlockSpec((STEPS, block, 128), lambda i: (0, i, 0))
    shape = jax.ShapeDtypeStruct((STEPS, tracers, 128), jnp.bfloat16)
    return pl.pallas_call(
        edge_rows,
        grid=(tracers // block,),
        in_specs=[pl.BlockSpec((4 * block, 128), lambda i: (i, 0))],
        out_specs=[half, half],
        out_shape=[shape, shape],
        name="edges",
    )(pulses)


def jacobian_body(pulse_ref, above_ref, below_ref, wind_x_ref, wind_y_ref, rows_ref, out_ref):
    count = out_ref.shape[1]
    field = (
        [above_ref[r].astype(jnp.float32) for r in range(STEPS)]
        + [pulse_ref[pl.ds(r, count, 4), :] for r in range(4)]
        + [below_ref[r].astype(jnp.float32) for r in range(STEPS)]
    )
    wind_x = wind_x_ref[...]
    wind_y = wind_y_ref[...]
    gain_x, loss_x = jnp.maximum(wind_x, 0.0), jnp.minimum(wind_x, 0.0)
    gain_y, loss_y = jnp.maximum(wind_y, 0.0), jnp.minimum(wind_y, 0.0)
    from_right = -pltpu.roll(loss_x, 127, 1)
    keep_x = 1.0 + loss_x - pltpu.roll(gain_x, 127, 1)
    first = 1
    for step in range(STEPS):
        new = []
        for i in range(len(field) - 2):
            w = first + i - 1
            here = field[i + 1]
            keep = keep_x[w : w + 1] + loss_y[w : w + 1] - gain_y[w + 1 : w + 2]
            new.append(
                keep * here
                + gain_x[w : w + 1] * pltpu.roll(here, 1, 1)
                + from_right[w : w + 1] * pltpu.roll(here, 127, 1)
                + gain_y[w : w + 1] * field[i]
                - loss_y[w + 1 : w + 2] * field[i + 2]
            )
        field = new
        first += 1
    sampled = jnp.concatenate([f.astype(jnp.bfloat16) for f in field], axis=1)
    out_ref[...] = lax.dot_general(
        rows_ref[...], sampled, (((1,), (1,)), ((), ())), preferred_element_type=jnp.float32
    ).astype(jnp.bfloat16)


def jacobian(pulses, above, below, wind_x, wind_y, rows, block=128):
    tracers = pulses.shape[0] // 4
    slots = rows.shape[0]
    halo = pl.BlockSpec((STEPS, block, 128), lambda i: (0, i, 0))
    return pl.pallas_call(
        jacobian_body,
        grid=(tracers // block,),
        in_specs=[
            pl.BlockSpec((4 * block, 128), lambda i: (i, 0)),
            halo,
            halo,
            pl.BlockSpec((8, 128), lambda i: (0, 0)),
            pl.BlockSpec((16, 128), lambda i: (0, 0)),
            pl.BlockSpec((slots, 512), lambda i: (0, 0)),
        ],
        out_specs=pl.BlockSpec((slots, block), lambda i: (0, i)),
        out_shape=jax.ShapeDtypeStruct((slots, tracers), jnp.bfloat16),
        name="jacobian",
    )(pulses, above, below, wind_x, wind_y, rows)


def on_device(pulses, wind_x, wind_y, obs_tile, obs_weight, obs_precision):
    tracers = pulses.shape[0]
    cells = lax.axis_size(CELLS)
    obs = obs_tile.shape[0]
    pulses = pulses.reshape(tracers * 4, 128)

    first, last = edges(pulses)
    winds = jnp.concatenate([wind_x, wind_y], axis=0)
    above = shifted(last, CELLS, 1)
    below = shifted(first, CELLS, -1)
    winds_above = shifted(winds, CELLS, 1)
    winds_below = shifted(winds, CELLS, -1)
    wide_x = jnp.concatenate([winds_above[2:4], wind_x, winds_below[0:2]], axis=0)
    wide_y = jnp.concatenate(
        [winds_above[6:8], wind_y, winds_below[4:7], jnp.zeros((7, 128), jnp.float32)], axis=0
    )

    tile = obs_tile[:, 0]
    order = jnp.arange(obs)
    earlier = (tile[:, None] == tile[None, :]) & (order[None, :] < order[:, None])
    slot = tile * CAP + jnp.sum(earlier.astype(jnp.int32), axis=1)
    chosen = (slot[:, None] == jnp.arange(cells * CAP)[None, :]).astype(jnp.bfloat16)
    wide = obs_weight.astype(jnp.float32)
    averaging = (wide / jnp.sum(wide, axis=1, keepdims=True)).astype(jnp.bfloat16)
    rows_out = lax.dot_general(
        chosen, averaging, (((0,), (0,)), ((), ())), preferred_element_type=jnp.float32
    ).astype(jnp.bfloat16)
    rows_in = exchanged(rows_out.reshape(cells, CAP, 512), CELLS).reshape(cells * CAP, 512)

    jac_tile = jacobian(pulses, above, below, wide_x, wide_y, rows_in)
    jac_back = exchanged(jac_tile.reshape(cells, CAP, tracers), CELLS)
    jac = lax.dot_general(
        chosen,
        jac_back.reshape(cells * CAP, tracers),
        (((1,), (0,)), ((), ())),
        preferred_element_type=jnp.float32,
    )
    weighted = (obs_precision.astype(jnp.float32)[:, None] * jac).astype(jnp.bfloat16)
    jac = jac.astype(jnp.bfloat16)

    group = lax.axis_size(XY)
    cols = exchanged(jnp.broadcast_to(weighted, (group,) + weighted.shape), XY)
    both = exchanged(jnp.broadcast_to(jac, (2,) + jac.shape), "xh")
    four = exchanged(jnp.broadcast_to(both, (2,) + both.shape), "core").reshape(2, 2, obs, tracers)
    blocks = four.reshape(2, 2, obs, 2, tracers // 2).transpose(1, 0, 3, 2, 4)
    rows = exchanged(blocks.reshape(group, obs, tracers // 2), XY)

    partial = lax.dot_general(
        rows.reshape(group * obs, tracers // 2),
        cols.reshape(group * obs, tracers),
        (((0,), (0,)), ((), ())),
        preferred_element_type=jnp.float32,
    ).astype(jnp.bfloat16)
    depth = lax.axis_size("z")
    parts = exchanged(partial.reshape(depth, tracers // 2 // depth, tracers), "z")
    return jnp.sum(parts.astype(jnp.float32), axis=0)


def solution(mesh):
    fine = Mesh(mesh.devices.reshape(2, 4, 8, 2, 2), CELLS + TRACERS)
    placed = (
        P(TRACERS, CELLS, None),
        P(CELLS, None),
        P(CELLS, None),
        P(CELLS, None),
        P(CELLS, None),
        P(CELLS),
    )
    return jax.shard_map(
        on_device, mesh=fine, in_specs=placed, out_specs=P(CELLS, TRACERS), check_vma=False
    )
```

```python
import jax
import jax.numpy as jnp
from jax import lax
from jax.experimental import pallas as pl
from jax.experimental.pallas import tpu as pltpu
from jax.sharding import Mesh, PartitionSpec as P

STEPS = 3
CAP = 4
XY = ("xl", "y")
CELLS = ("xl", "y", "z")
TRACERS = ("xh", "core")
PLANE = XY + TRACERS


def shifted(value, axis, steps):
    count = lax.axis_size(axis)
    return lax.ppermute(value, axis, [(i, (i + steps) % count) for i in range(count)])


def exchanged(value, axis):
    return lax.all_to_all(value, axis, split_axis=0, concat_axis=0, tiled=True)


def edge_rows(pulse_ref, wind_x_ref, wind_y_ref, first_ref, last_ref):
    count = pulse_ref.shape[0] // 4
    rows = [pulse_ref[pl.ds(r, count, 4), :].astype(jnp.bfloat16) for r in range(4)]
    for r in range(STEPS):
        first_ref[r * count : (r + 1) * count] = rows[r]
        last_ref[r * count : (r + 1) * count] = rows[r + 1]
    winds = jnp.concatenate([wind_x_ref[...], wind_y_ref[...]], axis=0)
    coarse = winds.astype(jnp.bfloat16)
    fine = (winds - coarse.astype(jnp.float32)).astype(jnp.bfloat16)
    both = jnp.concatenate([coarse.astype(jnp.float32), fine.astype(jnp.float32)], axis=0)
    first_ref[STEPS * count :] = both.astype(jnp.bfloat16)
    last_ref[STEPS * count :] = both.astype(jnp.bfloat16)


def edges(pulses, wind_x, wind_y):
    tracers = pulses.shape[0] // 4
    shape = jax.ShapeDtypeStruct((STEPS * tracers + 16, 128), jnp.bfloat16)
    return pl.pallas_call(edge_rows, out_shape=[shape, shape], name="edges")(
        pulses, wind_x, wind_y
    )


PIECE = 16


def jacobian_body(
    pulse_ref, a0, a1, a2, a_winds, b0, b1, b2, b_winds, wind_x_ref, wind_y_ref, rows_ref,
    out_ref, coef_ref, sampled_ref,
):
    count = out_ref.shape[2]

    @pl.when(pl.program_id(0) == 0)
    def _():
        above = a_winds[...].astype(jnp.float32)
        below = b_winds[...].astype(jnp.float32)
        above = above[0:8] + above[8:16]
        below = below[0:8] + below[8:16]
        wind_x = jnp.concatenate([above[2:4], wind_x_ref[...], below[0:2]], axis=0)
        wind_y = jnp.concatenate([above[6:8], wind_y_ref[...], below[4:6]], axis=0)
        next_y = jnp.concatenate([above[7:8], wind_y_ref[...], below[4:7]], axis=0)
        gain_x, loss_x = jnp.maximum(wind_x, 0.0), jnp.minimum(wind_x, 0.0)
        gain_y, loss_y = jnp.maximum(wind_y, 0.0), jnp.minimum(wind_y, 0.0)
        keep = 1.0 + loss_x - pltpu.roll(gain_x, 127, 1) + loss_y - jnp.maximum(next_y, 0.0)
        parts = [
            keep, gain_x, -pltpu.roll(loss_x, 127, 1), gain_y, -jnp.minimum(next_y, 0.0)
        ]
        for k, part in enumerate(parts):
            for w in range(8):
                coef_ref[k * 8 + w] = jnp.broadcast_to(part[w : w + 1], (PIECE, 128))

    for piece in range(count // PIECE):
        at = piece * PIECE
        field = (
            [ref[at : at + PIECE].astype(jnp.float32) for ref in (a0, a1, a2)]
            + [pulse_ref[pl.ds(4 * at + r, PIECE, 4), :] for r in range(4)]
            + [ref[at : at + PIECE].astype(jnp.float32) for ref in (b0, b1, b2)]
        )
        for step in range(STEPS):
            new = []
            for i in range(len(field) - 2):
                w = step + i
                here = field[i + 1]
                new.append(
                    coef_ref[w] * here
                    + coef_ref[8 + w] * pltpu.roll(here, 1, 1)
                    + coef_ref[16 + w] * pltpu.roll(here, 127, 1)
                    + coef_ref[24 + w] * field[i]
                    + coef_ref[32 + w] * field[i + 2]
                )
            field = new
        for r in range(4):
            sampled_ref[at : at + PIECE, r * 128 : (r + 1) * 128] = field[r].astype(jnp.bfloat16)
    jac = lax.dot_general(
        rows_ref[...],
        sampled_ref[...],
        (((1,), (1,)), ((), ())),
        preferred_element_type=jnp.float32,
    )
    out_ref[...] = jac.reshape(out_ref.shape).astype(jnp.bfloat16)


def jacobian(pulses, above, below, wind_x, wind_y, rows, block=128):
    tracers = pulses.shape[0] // 4
    slots = rows.shape[0]
    steps = tracers // block
    halo = [
        pl.BlockSpec((block, 128), lambda i, r=r: (r * steps + i, 0)) for r in range(STEPS)
    ] + [pl.BlockSpec((16, 128), lambda i: (STEPS * tracers // 16, 0))]
    wind = pl.BlockSpec((4, 128), lambda i: (0, 0))
    return pl.pallas_call(
        jacobian_body,
        grid=(steps,),
        in_specs=[pl.BlockSpec((4 * block, 128), lambda i: (i, 0))]
        + halo
        + halo
        + [wind, wind, pl.BlockSpec((slots, 512), lambda i: (0, 0))],
        out_specs=pl.BlockSpec((slots // CAP, CAP, block), lambda i: (0, 0, i)),
        out_shape=jax.ShapeDtypeStruct((slots // CAP, CAP, tracers), jnp.bfloat16),
        scratch_shapes=[
            pltpu.VMEM((40, PIECE, 128), jnp.float32),
            pltpu.VMEM((block, 512), jnp.bfloat16),
        ],
        name="jacobian",
    )(pulses, *[above] * 4, *[below] * 4, wind_x, wind_y, rows)


def gram_body(place_ref, own_ref, across_ref, other_ref, cols_ref, out_ref, rows_ref):
    block = own_ref.shape[0] // 2

    @pl.when(pl.program_id(0) == 0)
    def _():
        parts = [own_ref[...], across_ref[...], other_ref[: 2 * block], other_ref[2 * block :]]
        for k, part in enumerate(parts):
            for s in range(2):
                at = pl.multiple_of(place_ref[2 * k + s] * block, block)
                rows_ref[pl.ds(at, block), :] = part[s * block : (s + 1) * block]

    cols = cols_ref[...]
    out_ref[...] = lax.dot_general(
        rows_ref[...],
        cols.reshape(cols.shape[0] * cols.shape[1], cols.shape[2]),
        (((0,), (0,)), ((), ())),
        preferred_element_type=jnp.float32,
    ).astype(jnp.bfloat16)


def gram_tile(place, own, across, other, cols, block=512):
    group, obs, tracers = cols.shape
    width = own.shape[1]
    whole = lambda v: pl.BlockSpec(v.shape, lambda i: (0, 0))
    return pl.pallas_call(
        gram_body,
        grid=(tracers // block,),
        in_specs=[
            pl.BlockSpec(memory_space=pltpu.SMEM),
            whole(own),
            whole(across),
            whole(other),
            pl.BlockSpec((group, obs, block), lambda i: (0, 0, i)),
        ],
        out_specs=pl.BlockSpec((width, block), lambda i: (0, i)),
        out_shape=jax.ShapeDtypeStruct((width, tracers), jnp.bfloat16),
        scratch_shapes=[pltpu.VMEM((group * obs, width), jnp.bfloat16)],
        name="gram",
    )(place, own, across, other, cols)


def on_device(pulses, wind_x, wind_y, obs_tile, obs_weight, obs_precision):
    tracers = pulses.shape[0]
    cells = lax.axis_size(CELLS)
    obs = obs_tile.shape[0]
    pulses = pulses.reshape(tracers * 4, 128)

    first, last = edges(pulses, wind_x, wind_y)
    above = shifted(last, CELLS, 1)
    below = shifted(first, CELLS, -1)

    tile = obs_tile[:, 0]
    order = jnp.arange(obs)
    earlier = (tile[:, None] == tile[None, :]) & (order[None, :] < order[:, None])
    slot = tile * CAP + jnp.sum(earlier.astype(jnp.int32), axis=1)
    chosen = (slot[:, None] == jnp.arange(cells * CAP)[None, :]).astype(jnp.bfloat16)
    wide = obs_weight.astype(jnp.float32)
    averaging = (wide / jnp.sum(wide, axis=1, keepdims=True)).astype(jnp.bfloat16)
    rows_out = lax.dot_general(
        chosen, averaging, (((0,), (0,)), ((), ())), preferred_element_type=jnp.float32
    ).astype(jnp.bfloat16)
    rows_in = exchanged(rows_out.reshape(cells, CAP, 512), CELLS).reshape(cells * CAP, 512)

    jac_tile = jacobian(pulses, above, below, wind_x, wind_y, rows_in)
    jac_back = exchanged(jac_tile, CELLS)
    jac = lax.dot_general(
        chosen,
        jac_back.reshape(cells * CAP, tracers),
        (((1,), (0,)), ((), ())),
        preferred_element_type=jnp.float32,
    )
    weighted = (obs_precision.astype(jnp.float32)[:, None] * jac).astype(jnp.bfloat16)
    jac = jac.astype(jnp.bfloat16)

    group = lax.axis_size(XY)
    peers = lax.axis_size(TRACERS)
    cols = exchanged(jnp.broadcast_to(weighted, (group,) + weighted.shape), XY)

    half = tracers // 2
    odd = lax.axis_index(XY) % 2
    low, high = jac[:, :half], jac[:, half:]
    same = jnp.where(odd == 0, low, high)
    cross = jnp.where(odd == 0, high, low)
    pairs = [(i // peers, i % peers) for i in range(group * peers)]
    to_same = [(a * peers + q, (2 * q + a % 2) * peers + a // 2) for a, q in pairs]
    to_cross = [(a * peers + q, (2 * q + 1 - a % 2) * peers + a // 2) for a, q in pairs]
    own = jnp.concatenate(
        [lax.ppermute(same, PLANE, to_same), lax.ppermute(cross, PLANE, to_cross)], axis=0
    )
    across = shifted(own, "xh", 1)
    other = shifted(jnp.concatenate([own, across], axis=0), "core", 1)
    tracer = lax.axis_index(TRACERS)
    place = jnp.stack(
        [2 * (tracer ^ flip) + (odd ^ s) for flip in (0, 2, 1, 3) for s in (0, 1)]
    ).astype(jnp.int32)

    partial = gram_tile(place, own, across, other, cols)
    depth = lax.axis_size("z")
    parts = exchanged(partial.reshape(depth, half // depth, tracers), "z")
    return jnp.sum(parts.astype(jnp.float32), axis=0)


def solution(mesh):
    fine = Mesh(mesh.devices.reshape(2, 4, 8, 2, 2), CELLS + TRACERS)
    placed = (
        P(TRACERS, CELLS, None),
        P(CELLS, None),
        P(CELLS, None),
        P(CELLS, None),
        P(CELLS, None),
        P(CELLS),
    )
    return jax.shard_map(
        on_device, mesh=fine, in_specs=placed, out_specs=P(CELLS, TRACERS), check_vma=False
    )
```

```python
import jax
import jax.numpy as jnp
from jax import lax
from jax.experimental import pallas as pl
from jax.experimental.pallas import tpu as pltpu
from jax.sharding import Mesh, PartitionSpec as P


STEPS = 3
GRANT = 16 * 1024 * 1024
CAP = 4
XY = ("xl", "y")
CELLS = ("xl", "y", "z")
TRACERS = ("xh", "core")
PLANE = XY + TRACERS


def shifted(value, axis, steps):
    count = lax.axis_size(axis)
    return lax.ppermute(value, axis, [(i, (i + steps) % count) for i in range(count)])


def exchanged(value, axis):
    return lax.all_to_all(value, axis, split_axis=0, concat_axis=0, tiled=True)


def edge_rows(pulse_ref, wind_x_ref, wind_y_ref, first_ref, last_ref):
    count = pulse_ref.shape[0] // 4
    rows = [pulse_ref[pl.ds(r, count, 4), :].astype(jnp.bfloat16) for r in range(4)]
    for r in range(STEPS):
        first_ref[r * count : (r + 1) * count] = rows[r]
        last_ref[r * count : (r + 1) * count] = rows[r + 1]
    winds = jnp.concatenate([wind_x_ref[...], wind_y_ref[...]], axis=0)
    coarse = winds.astype(jnp.bfloat16)
    fine = (winds - coarse.astype(jnp.float32)).astype(jnp.bfloat16)
    both = jnp.concatenate([coarse.astype(jnp.float32), fine.astype(jnp.float32)], axis=0)
    first_ref[STEPS * count :] = both.astype(jnp.bfloat16)
    last_ref[STEPS * count :] = both.astype(jnp.bfloat16)


def edges(pulses, wind_x, wind_y):
    tracers = pulses.shape[0] // 4
    shape = jax.ShapeDtypeStruct((STEPS * tracers + 16, 128), jnp.bfloat16)
    return pl.pallas_call(
        edge_rows,
        out_shape=[shape, shape],
        compiler_params=pltpu.CompilerParams(vmem_limit_bytes=GRANT),
        name="edges",
    )(pulses, wind_x, wind_y)


PIECE = 16


def transport_body(
    pulse_ref, a0, a1, a2, a_winds, b0, b1, b2, b_winds, wind_x_ref, wind_y_ref, out_ref, coef_ref
):
    count = out_ref.shape[0]

    @pl.when(pl.program_id(0) == 0)
    def _():
        above = a_winds[...].astype(jnp.float32)
        below = b_winds[...].astype(jnp.float32)
        above = above[0:8] + above[8:16]
        below = below[0:8] + below[8:16]
        wind_x = jnp.concatenate([above[2:4], wind_x_ref[...], below[0:2]], axis=0)
        wind_y = jnp.concatenate([above[6:8], wind_y_ref[...], below[4:6]], axis=0)
        next_y = jnp.concatenate([above[7:8], wind_y_ref[...], below[4:7]], axis=0)
        gain_x, loss_x = jnp.maximum(wind_x, 0.0), jnp.minimum(wind_x, 0.0)
        gain_y, loss_y = jnp.maximum(wind_y, 0.0), jnp.minimum(wind_y, 0.0)
        keep = 1.0 + loss_x - pltpu.roll(gain_x, 127, 1) + loss_y - jnp.maximum(next_y, 0.0)
        parts = [
            keep, gain_x, -pltpu.roll(loss_x, 127, 1), gain_y, -jnp.minimum(next_y, 0.0)
        ]
        for k, part in enumerate(parts):
            for w in range(8):
                coef_ref[k * 8 + w] = jnp.broadcast_to(part[w : w + 1], (PIECE, 128))

    for piece in range(count // PIECE):
        at = piece * PIECE
        field = (
            [ref[at : at + PIECE].astype(jnp.float32) for ref in (a0, a1, a2)]
            + [pulse_ref[pl.ds(4 * at + r, PIECE, 4), :] for r in range(4)]
            + [ref[at : at + PIECE].astype(jnp.float32) for ref in (b0, b1, b2)]
        )
        for step in range(STEPS):
            new = []
            for i in range(len(field) - 2):
                w = step + i
                here = field[i + 1]
                new.append(
                    coef_ref[w] * here
                    + coef_ref[8 + w] * pltpu.roll(here, 1, 1)
                    + coef_ref[16 + w] * pltpu.roll(here, 127, 1)
                    + coef_ref[24 + w] * field[i]
                    + coef_ref[32 + w] * field[i + 2]
                )
            field = new
        for r in range(4):
            out_ref[at : at + PIECE, r * 128 : (r + 1) * 128] = field[r].astype(jnp.bfloat16)


def transport(pulses, above, below, wind_x, wind_y, block=256):
    tracers = pulses.shape[0] // 4
    steps = tracers // block
    halo = [
        pl.BlockSpec((block, 128), lambda i, r=r: (r * steps + i, 0)) for r in range(STEPS)
    ] + [pl.BlockSpec((16, 128), lambda i: (STEPS * tracers // 16, 0))]
    wind = pl.BlockSpec((4, 128), lambda i: (0, 0))
    return pl.pallas_call(
        transport_body,
        grid=(steps,),
        in_specs=[pl.BlockSpec((4 * block, 128), lambda i: (i, 0))] + halo + halo + [wind, wind],
        out_specs=pl.BlockSpec((block, 512), lambda i: (i, 0)),
        out_shape=jax.ShapeDtypeStruct((tracers, 512), jnp.bfloat16),
        scratch_shapes=[pltpu.VMEM((40, PIECE, 128), jnp.float32)],
        compiler_params=pltpu.CompilerParams(vmem_limit_bytes=GRANT),
        name="transport",
    )(pulses, *[above] * 4, *[below] * 4, wind_x, wind_y)


def jacobian_body(rows_ref, low_ref, high_ref, out_ref, full_ref):
    @pl.when(pl.program_id(0) == 0)
    def _():
        count, width = rows_ref.shape
        mine = rows_ref[...].astype(jnp.float32).reshape(count // 8, 8, width)
        swap = pltpu.roll(mine, 4, 1)
        top = lax.broadcasted_iota(jnp.int32, mine.shape, 1) < 4
        left = jnp.where(top, mine, swap).reshape(count, width)
        right = jnp.where(top, swap, mine).reshape(count, width)
        full_ref[:, :width] = left.astype(jnp.bfloat16)
        full_ref[:, width:] = right.astype(jnp.bfloat16)

    dims = (((1,), (1,)), ((), ()))
    full = full_ref[...]
    low = lax.dot_general(full, low_ref[...], dims, preferred_element_type=jnp.float32)
    high = lax.dot_general(full, high_ref[...], dims, preferred_element_type=jnp.float32)
    row = lax.broadcasted_iota(jnp.int32, low.shape, 0)
    out_ref[...] = jnp.where((row & 4) == 0, low, high).astype(jnp.bfloat16)


def jacobian(rows, sampled, block=256):
    tracers = sampled.shape[0]
    count, width = rows.shape
    steps = tracers // 2 // block
    return pl.pallas_call(
        jacobian_body,
        grid=(steps,),
        in_specs=[
            pl.BlockSpec((count, width), lambda i: (0, 0)),
            pl.BlockSpec((block, 512), lambda i: (i, 0)),
            pl.BlockSpec((block, 512), lambda i: (steps + i, 0)),
        ],
        out_specs=pl.BlockSpec((count, block), lambda i: (0, i)),
        out_shape=jax.ShapeDtypeStruct((count, tracers // 2), jnp.bfloat16),
        scratch_shapes=[pltpu.VMEM((count, 2 * width), jnp.bfloat16)],
        compiler_params=pltpu.CompilerParams(vmem_limit_bytes=GRANT),
        name="jacobian",
    )(rows, sampled, sampled)


def gram_body(place_ref, same_ref, cross_ref, across_ref, other_ref, *refs):
    cols, out_ref, rows_ref, cols_ref = refs[:-3], refs[-3], refs[-2], refs[-1]
    block = same_ref.shape[0]

    @pl.when(pl.program_id(0) == 0)
    def _():
        parts = [same_ref[...], cross_ref[...]]
        for ref in (across_ref, other_ref):
            parts += [ref[s : s + block] for s in range(0, ref.shape[0], block)]
        for k, part in enumerate(parts):
            at = pl.multiple_of(place_ref[k] * block, block)
            rows_ref[:, pl.ds(at, block)] = part.T

    for k, ref in enumerate(cols):
        at = pl.multiple_of(place_ref[8 + k] * block, block)
        cols_ref[pl.ds(at, block), :] = ref[...]
    out_ref[...] = lax.dot_general(
        rows_ref[...], cols_ref[...], (((1,), (0,)), ((), ())), preferred_element_type=jnp.float32
    ).astype(jnp.bfloat16)


def gram_tile(place, same, cross, across, other, cols, block=256):
    obs, tracers = cols[0].shape
    width = same.shape[1]
    whole = lambda v: pl.BlockSpec(v.shape, lambda i: (0, 0))
    return pl.pallas_call(
        gram_body,
        grid=(tracers // block,),
        in_specs=[pl.BlockSpec(memory_space=pltpu.SMEM)]
        + [whole(v) for v in (same, cross, across, other)]
        + [pl.BlockSpec((obs, block), lambda i: (0, i))] * len(cols),
        out_specs=pl.BlockSpec((width, block), lambda i: (0, i)),
        out_shape=jax.ShapeDtypeStruct((width, tracers), jnp.bfloat16),
        scratch_shapes=[
            pltpu.VMEM((width, len(cols) * obs), jnp.bfloat16),
            pltpu.VMEM((len(cols) * obs, block), jnp.bfloat16),
        ],
        compiler_params=pltpu.CompilerParams(vmem_limit_bytes=GRANT),
        name="gram",
    )(place, same, cross, across, other, *cols)


def on_device(pulses, wind_x, wind_y, obs_tile, obs_weight, obs_precision):
    tracers = pulses.shape[0]
    cells = lax.axis_size(CELLS)
    obs = obs_tile.shape[0]
    half = tracers // 2
    pulses = pulses.reshape(tracers * 4, 128)

    first, last = edges(pulses, wind_x, wind_y)
    above = shifted(last, CELLS, 1)
    below = shifted(first, CELLS, -1)
    sampled = transport(pulses, above, below, wind_x, wind_y)

    tile = obs_tile[:, 0]
    order = jnp.arange(obs)
    earlier = (tile[:, None] == tile[None, :]) & (order[None, :] < order[:, None])
    slot = 2 * CAP * tile + jnp.sum(earlier.astype(jnp.int32), axis=1)
    lanes = jnp.arange(2 * CAP * cells)[None, :]
    chosen = [(slot[:, None] + CAP * h == lanes).astype(jnp.bfloat16) for h in range(2)]
    wide = obs_weight.astype(jnp.float32)
    averaging = (wide / jnp.sum(wide, axis=1, keepdims=True)).astype(jnp.bfloat16)
    split = obs_weight.shape[1] // 2
    rows_out = lax.dot_general(
        jnp.concatenate(chosen, axis=0),
        jnp.concatenate([averaging[:, :split], averaging[:, split:]], axis=0),
        (((0,), (0,)), ((), ())),
        preferred_element_type=jnp.float32,
    ).astype(jnp.bfloat16)
    rows_in = exchanged(rows_out.reshape(cells, 2 * CAP, split), CELLS)

    jac_tile = jacobian(rows_in.reshape(cells * 2 * CAP, split), sampled)
    jac_back = exchanged(jac_tile.reshape(cells, 2 * CAP, half), CELLS)
    jac_back = jac_back.reshape(cells * 2 * CAP, half)
    jac = [
        lax.dot_general(
            c, jac_back, (((1,), (0,)), ((), ())), preferred_element_type=jnp.float32
        )
        for c in chosen
    ]
    precision = obs_precision.astype(jnp.float32)[:, None]
    weighted = jnp.concatenate([precision * j for j in jac], axis=1).astype(jnp.bfloat16)
    low, high = [j.astype(jnp.bfloat16) for j in jac]

    group = lax.axis_size(XY)
    peers = lax.axis_size(TRACERS)
    here = lax.axis_index(XY)
    odd = here % 2
    pairs = [(i // peers, i % peers) for i in range(group * peers)]
    to_same = [(a * peers + q, (2 * q + a % 2) * peers + a // 2) for a, q in pairs]
    to_cross = [(a * peers + q, (2 * q + 1 - a % 2) * peers + a // 2) for a, q in pairs]
    same = lax.ppermute(jnp.where(odd == 0, low, high), PLANE, to_same)
    cross = lax.ppermute(jnp.where(odd == 0, high, low), PLANE, to_cross)
    across = shifted(jnp.concatenate([same, cross], axis=0), "xh", 1)
    other = shifted(jnp.concatenate([same, cross, across], axis=0), "core", 1)

    beside = shifted(weighted, "xl", 1)
    deep = lax.axis_size("y")
    cols = [weighted, beside]
    for value in (weighted, beside):
        for d in range(1, deep):
            cols.append(shifted(value, "y", d))
    xl, y = lax.axis_index("xl"), lax.axis_index("y")
    owners = [here, (1 - xl) * deep + y]
    owners += [xl * deep + (y - d) % deep for d in range(1, deep)]
    owners += [(1 - xl) * deep + (y - d) % deep for d in range(1, deep)]
    tracer = lax.axis_index(TRACERS)
    row_owners = [2 * (tracer ^ flip) + (odd ^ s) for flip in (0, 2, 1, 3) for s in (0, 1)]
    place = jnp.stack(row_owners + owners).astype(jnp.int32)

    partial = gram_tile(place, same, cross, across, other, cols)
    depth = lax.axis_size("z")
    parts = exchanged(partial.reshape(depth, half // depth, tracers), "z")
    return jnp.sum(parts.astype(jnp.float32), axis=0)


def solution(mesh):
    fine = Mesh(mesh.devices.reshape(2, 4, 8, 2, 2), CELLS + TRACERS)
    placed = (
        P(TRACERS, CELLS, None),
        P(CELLS, None),
        P(CELLS, None),
        P(CELLS, None),
        P(CELLS, None),
        P(CELLS),
    )
    return jax.shard_map(
        on_device, mesh=fine, in_specs=placed, out_specs=P(CELLS, TRACERS), check_vma=False
    )
```

```python
import jax
import jax.numpy as jnp
from jax import lax
from jax.experimental import pallas as pl
from jax.experimental.pallas import tpu as pltpu
from jax.sharding import Mesh, PartitionSpec as P


STEPS = 3
GRANT = 16 * 1024 * 1024
CAP = 4
XY = ("xl", "y")
CELLS = ("xl", "y", "z")
TRACERS = ("xh", "core")
PLANE = XY + TRACERS


def shifted(value, axis, steps):
    count = lax.axis_size(axis)
    return lax.ppermute(value, axis, [(i, (i + steps) % count) for i in range(count)])


def exchanged(value, axis):
    return lax.all_to_all(value, axis, split_axis=0, concat_axis=0, tiled=True)


def edge_rows(pulse_ref, wind_x_ref, wind_y_ref, *out_refs):
    tracers = pulse_ref.shape[0] // 4
    rows = [pulse_ref[pl.ds(r, tracers, 4), :].astype(jnp.bfloat16) for r in range(4)]
    winds = jnp.concatenate([wind_x_ref[...], wind_y_ref[...]], axis=0)
    coarse = winds.astype(jnp.bfloat16).astype(jnp.float32)
    both = jnp.concatenate([coarse, winds - coarse], axis=0).astype(jnp.bfloat16)
    for k, (start, size) in enumerate(spans(tracers)):
        for edge in range(2):
            ref = out_refs[2 * k + edge]
            for r in range(STEPS):
                ref[r * size : (r + 1) * size] = rows[r + edge][start : start + size]
            ref[STEPS * size :] = both


def spans(tracers):
    cut = tracers * 5 // 8
    return [(0, cut), (cut, tracers - cut)]


def edges(pulses, wind_x, wind_y):
    tracers = pulses.shape[0] // 4
    shapes = []
    for start, size in spans(tracers):
        shapes += [jax.ShapeDtypeStruct((STEPS * size + 16, 128), jnp.bfloat16)] * 2
    return pl.pallas_call(edge_rows, out_shape=shapes, name="edges")(pulses, wind_x, wind_y)


PIECE = 16


def transport_body(
    pulse_ref, a0, a1, a2, b0, b1, b2, a_winds, b_winds, wind_x_ref, wind_y_ref, *refs
):
    out_ref, coef_ref = refs[-2:]
    count = out_ref.shape[0]

    @pl.when(pl.program_id(0) == 0)
    def _():
        above = a_winds[...].astype(jnp.float32)
        below = b_winds[...].astype(jnp.float32)
        above = above[0:8] + above[8:16]
        below = below[0:8] + below[8:16]
        wind_x = jnp.concatenate([above[2:4], wind_x_ref[...], below[0:2]], axis=0)
        wind_y = jnp.concatenate([above[6:8], wind_y_ref[...], below[4:6]], axis=0)
        next_y = jnp.concatenate([above[7:8], wind_y_ref[...], below[4:7]], axis=0)
        gain_x, loss_x = jnp.maximum(wind_x, 0.0), jnp.minimum(wind_x, 0.0)
        gain_y, loss_y = jnp.maximum(wind_y, 0.0), jnp.minimum(wind_y, 0.0)
        keep = 1.0 + loss_x - pltpu.roll(gain_x, 127, 1) + loss_y - jnp.maximum(next_y, 0.0)
        parts = [
            keep, gain_x, -pltpu.roll(loss_x, 127, 1), gain_y, -jnp.minimum(next_y, 0.0)
        ]
        for k, part in enumerate(parts):
            for w in range(8):
                coef_ref[k * 8 + w] = jnp.broadcast_to(part[w : w + 1], (PIECE, 128))

    for piece in range(count // PIECE):
        at = piece * PIECE
        field = (
            [ref[at : at + PIECE].astype(jnp.float32) for ref in (a0, a1, a2)]
            + [pulse_ref[pl.ds(4 * at + r, PIECE, 4), :] for r in range(4)]
            + [ref[at : at + PIECE].astype(jnp.float32) for ref in (b0, b1, b2)]
        )
        for step in range(STEPS):
            new = []
            for i in range(len(field) - 2):
                w = step + i
                here = field[i + 1]
                new.append(
                    coef_ref[w] * here
                    + coef_ref[8 + w] * pltpu.roll(here, 1, 1)
                    + coef_ref[16 + w] * pltpu.roll(here, 127, 1)
                    + coef_ref[24 + w] * field[i]
                    + coef_ref[32 + w] * field[i + 2]
                )
            field = new
        for r in range(4):
            out_ref[at : at + PIECE, r * 128 : (r + 1) * 128] = field[r].astype(jnp.bfloat16)


def transport(pulses, above, below, wind_x, wind_y, span, into=None, block=128):
    tracers = pulses.shape[0] // 4
    start, size = span
    skip, steps = start // block, size // block
    halo = [
        pl.BlockSpec((block, 128), lambda i, r=r: (r * steps + i, 0)) for r in range(STEPS)
    ]
    last = [pl.BlockSpec((16, 128), lambda i: (STEPS * size // 16, 0))] * 2
    wind = pl.BlockSpec((4, 128), lambda i: (0, 0))
    operands = [pulses, *[above] * 3, *[below] * 3, above, below, wind_x, wind_y]
    specs = [pl.BlockSpec((4 * block, 128), lambda i: (skip + i, 0))] + halo + halo + last
    specs += [wind, wind]
    aliases = {}
    if into is not None:
        aliases = {len(operands): 0}
        operands.append(into)
        specs.append(pl.BlockSpec(memory_space=pl.ANY))
    return pl.pallas_call(
        transport_body,
        grid=(steps,),
        in_specs=specs,
        out_specs=pl.BlockSpec((block, 512), lambda i: (skip + i, 0)),
        out_shape=jax.ShapeDtypeStruct((tracers, 512), jnp.bfloat16),
        scratch_shapes=[pltpu.VMEM((40, PIECE, 128), jnp.float32)],
        input_output_aliases=aliases,
        compiler_params=pltpu.CompilerParams(vmem_limit_bytes=GRANT),
        name="transport",
    )(*operands)


def jacobian_body(rows_ref, low_ref, high_ref, out_ref, full_ref):
    @pl.when(pl.program_id(0) == 0)
    def _():
        count, width = rows_ref.shape
        mine = rows_ref[...].astype(jnp.float32).reshape(count // 8, 8, width)
        swap = pltpu.roll(mine, 4, 1)
        top = lax.broadcasted_iota(jnp.int32, mine.shape, 1) < 4
        left = jnp.where(top, mine, swap).reshape(count, width)
        right = jnp.where(top, swap, mine).reshape(count, width)
        full_ref[:, :width] = left.astype(jnp.bfloat16)
        full_ref[:, width:] = right.astype(jnp.bfloat16)

    dims = (((1,), (1,)), ((), ()))
    full = full_ref[...]
    low = lax.dot_general(full, low_ref[...], dims, preferred_element_type=jnp.float32)
    high = lax.dot_general(full, high_ref[...], dims, preferred_element_type=jnp.float32)
    row = lax.broadcasted_iota(jnp.int32, low.shape, 0)
    out_ref[...] = jnp.where((row & 4) == 0, low, high).astype(jnp.bfloat16)


def jacobian(rows, sampled, block=256):
    tracers = sampled.shape[0]
    count, width = rows.shape
    steps = tracers // 2 // block
    return pl.pallas_call(
        jacobian_body,
        grid=(steps,),
        in_specs=[
            pl.BlockSpec((count, width), lambda i: (0, 0)),
            pl.BlockSpec((block, 512), lambda i: (i, 0)),
            pl.BlockSpec((block, 512), lambda i: (steps + i, 0)),
        ],
        out_specs=pl.BlockSpec((count, block), lambda i: (0, i)),
        out_shape=jax.ShapeDtypeStruct((count, tracers // 2), jnp.bfloat16),
        scratch_shapes=[pltpu.VMEM((count, 2 * width), jnp.bfloat16)],
        compiler_params=pltpu.CompilerParams(vmem_limit_bytes=GRANT),
        name="jacobian",
    )(rows, sampled, sampled)


def gram_body(place_ref, same_ref, cross_ref, across_ref, other_ref, *refs):
    cols, out_ref, rows_ref, cols_ref = refs[:-3], refs[-3], refs[-2], refs[-1]
    block = same_ref.shape[0]

    @pl.when(pl.program_id(0) == 0)
    def _():
        parts = [same_ref[...], cross_ref[...]]
        for ref in (across_ref, other_ref):
            parts += [ref[s : s + block] for s in range(0, ref.shape[0], block)]
        for k, part in enumerate(parts):
            at = pl.multiple_of(place_ref[k] * block, block)
            rows_ref[:, pl.ds(at, block)] = part.T

    for k, ref in enumerate(cols):
        at = pl.multiple_of(place_ref[8 + k] * block, block)
        cols_ref[pl.ds(at, block), :] = ref[...]
    out_ref[...] = lax.dot_general(
        rows_ref[...], cols_ref[...], (((1,), (0,)), ((), ())), preferred_element_type=jnp.float32
    ).astype(jnp.bfloat16)


def gram_tile(place, same, cross, across, other, cols, block=256):
    obs, tracers = cols[0].shape
    width = same.shape[1]
    whole = lambda v: pl.BlockSpec(v.shape, lambda i: (0, 0))
    return pl.pallas_call(
        gram_body,
        grid=(tracers // block,),
        in_specs=[pl.BlockSpec(memory_space=pltpu.SMEM)]
        + [whole(v) for v in (same, cross, across, other)]
        + [pl.BlockSpec((obs, block), lambda i: (0, i))] * len(cols),
        out_specs=pl.BlockSpec((width, block), lambda i: (0, i)),
        out_shape=jax.ShapeDtypeStruct((width, tracers), jnp.bfloat16),
        scratch_shapes=[
            pltpu.VMEM((width, len(cols) * obs), jnp.bfloat16),
            pltpu.VMEM((len(cols) * obs, block), jnp.bfloat16),
        ],
        compiler_params=pltpu.CompilerParams(vmem_limit_bytes=GRANT),
        name="gram",
    )(place, same, cross, across, other, *cols)


def on_device(pulses, wind_x, wind_y, obs_tile, obs_weight, obs_precision):
    tracers = pulses.shape[0]
    cells = lax.axis_size(CELLS)
    obs = obs_tile.shape[0]
    half = tracers // 2
    pulses = pulses.reshape(tracers * 4, 128)

    messages = edges(pulses, wind_x, wind_y)
    halos = []
    for k in range(2):
        halos.append((shifted(messages[2 * k + 1], CELLS, 1), shifted(messages[2 * k], CELLS, -1)))
    sampled = None
    for span, (above, below) in zip(spans(tracers), halos):
        sampled = transport(pulses, above, below, wind_x, wind_y, span, sampled)

    tile = obs_tile[:, 0]
    order = jnp.arange(obs)
    earlier = (tile[:, None] == tile[None, :]) & (order[None, :] < order[:, None])
    slot = 2 * CAP * tile + jnp.sum(earlier.astype(jnp.int32), axis=1)
    lanes = jnp.arange(2 * CAP * cells)[None, :]
    chosen = [(slot[:, None] + CAP * h == lanes).astype(jnp.bfloat16) for h in range(2)]
    wide = obs_weight.astype(jnp.float32)
    averaging = (wide / jnp.sum(wide, axis=1, keepdims=True)).astype(jnp.bfloat16)
    split = obs_weight.shape[1] // 2
    rows_out = lax.dot_general(
        jnp.concatenate(chosen, axis=0),
        jnp.concatenate([averaging[:, :split], averaging[:, split:]], axis=0),
        (((0,), (0,)), ((), ())),
        preferred_element_type=jnp.float32,
    ).astype(jnp.bfloat16)
    rows_in = exchanged(rows_out.reshape(cells, 2 * CAP, split), CELLS)

    jac_tile = jacobian(rows_in.reshape(cells * 2 * CAP, split), sampled)
    jac_back = exchanged(jac_tile.reshape(cells, 2 * CAP, half), CELLS)
    jac_back = jac_back.reshape(cells * 2 * CAP, half)
    jac = [
        lax.dot_general(
            c, jac_back, (((1,), (0,)), ((), ())), preferred_element_type=jnp.float32
        )
        for c in chosen
    ]
    precision = obs_precision.astype(jnp.float32)[:, None]
    weighted = jnp.concatenate([precision * j for j in jac], axis=1).astype(jnp.bfloat16)
    low, high = [j.astype(jnp.bfloat16) for j in jac]

    group = lax.axis_size(XY)
    peers = lax.axis_size(TRACERS)
    here = lax.axis_index(XY)
    odd = here % 2
    pairs = [(i // peers, i % peers) for i in range(group * peers)]
    to_same = [(a * peers + q, (2 * q + a % 2) * peers + a // 2) for a, q in pairs]
    to_cross = [(a * peers + q, (2 * q + 1 - a % 2) * peers + a // 2) for a, q in pairs]
    same = lax.ppermute(jnp.where(odd == 0, low, high), PLANE, to_same)
    cross = lax.ppermute(jnp.where(odd == 0, high, low), PLANE, to_cross)
    across = shifted(jnp.concatenate([same, cross], axis=0), "xh", 1)
    other = shifted(jnp.concatenate([same, cross, across], axis=0), "core", 1)

    beside = shifted(weighted, "xl", 1)
    deep = lax.axis_size("y")
    cols = [weighted, beside]
    for value in (weighted, beside):
        for d in range(1, deep):
            cols.append(shifted(value, "y", d))
    xl, y = lax.axis_index("xl"), lax.axis_index("y")
    owners = [here, (1 - xl) * deep + y]
    owners += [xl * deep + (y - d) % deep for d in range(1, deep)]
    owners += [(1 - xl) * deep + (y - d) % deep for d in range(1, deep)]
    tracer = lax.axis_index(TRACERS)
    row_owners = [2 * (tracer ^ flip) + (odd ^ s) for flip in (0, 2, 1, 3) for s in (0, 1)]
    place = jnp.stack(row_owners + owners).astype(jnp.int32)

    partial = gram_tile(place, same, cross, across, other, cols)
    depth = lax.axis_size("z")
    parts = exchanged(partial.reshape(depth, half // depth, tracers), "z")
    return jnp.sum(parts.astype(jnp.float32), axis=0)


def solution(mesh):
    fine = Mesh(mesh.devices.reshape(2, 4, 8, 2, 2), CELLS + TRACERS)
    placed = (
        P(TRACERS, CELLS, None),
        P(CELLS, None),
        P(CELLS, None),
        P(CELLS, None),
        P(CELLS, None),
        P(CELLS),
    )
    return jax.shard_map(
        on_device, mesh=fine, in_specs=placed, out_specs=P(CELLS, TRACERS), check_vma=False
    )
```

```python
import functools

import jax
import jax.numpy as jnp
from jax import lax
from jax.experimental import pallas as pl
from jax.experimental.pallas import tpu as pltpu
from jax.sharding import Mesh, PartitionSpec as P


STEPS = 3
GRANT = 16 * 1024 * 1024
CAP = 4
XY = ("xl", "y")
CELLS = ("xl", "y", "z")
TRACERS = ("xh", "core")
PLANE = XY + TRACERS


def shifted(value, axis, steps):
    count = lax.axis_size(axis)
    return lax.ppermute(value, axis, [(i, (i + steps) % count) for i in range(count)])


def exchanged(value, axis):
    return lax.all_to_all(value, axis, split_axis=0, concat_axis=0, tiled=True)


def edge_rows(pulse_ref, wind_x_ref, wind_y_ref, *out_refs):
    tracers = pulse_ref.shape[0] // 4
    rows = [pulse_ref[pl.ds(r, tracers, 4), :].astype(jnp.bfloat16) for r in range(4)]
    winds = jnp.concatenate([wind_x_ref[...], wind_y_ref[...]], axis=0)
    coarse = winds.astype(jnp.bfloat16).astype(jnp.float32)
    both = jnp.concatenate([coarse, winds - coarse], axis=0).astype(jnp.bfloat16)
    for k, (start, size) in enumerate(spans(tracers)):
        for edge in range(2):
            ref = out_refs[2 * k + edge]
            for r in range(STEPS):
                ref[r * size : (r + 1) * size] = rows[r + edge][start : start + size]
            ref[STEPS * size :] = both


def spans(tracers):
    cut = tracers * 5 // 8
    return [(0, cut), (cut, tracers - cut)]


def edges(pulses, wind_x, wind_y):
    tracers = pulses.shape[0] // 4
    shapes = []
    for start, size in spans(tracers):
        shapes += [jax.ShapeDtypeStruct((STEPS * size + 16, 128), jnp.bfloat16)] * 2
    return pl.pallas_call(edge_rows, out_shape=shapes, name="edges")(pulses, wind_x, wind_y)


PIECE = 16


def transport_body(
    skip, pulse_ref, a0, a1, a2, b0, b1, b2, a_winds, b_winds, wind_x_ref, wind_y_ref, *refs
):
    out_ref, coef_ref, fetched_ref, sems = refs[-4:]
    count = out_ref.shape[0]
    block = pl.program_id(0)

    def fetch(i):
        source = pulse_ref.at[pl.ds((skip + i) * 4 * count, 4 * count)]
        return pltpu.make_async_copy(source, fetched_ref.at[i % 2], sems.at[i % 2])

    @pl.when(block == 0)
    def _():
        fetch(block).start()

    @pl.when(block + 1 < pl.num_programs(0))
    def _():
        fetch(block + 1).start()

    @pl.when(pl.program_id(0) == 0)
    def _():
        above = a_winds[...].astype(jnp.float32)
        below = b_winds[...].astype(jnp.float32)
        above = above[0:8] + above[8:16]
        below = below[0:8] + below[8:16]
        wind_x = jnp.concatenate([above[2:4], wind_x_ref[...], below[0:2]], axis=0)
        wind_y = jnp.concatenate([above[6:8], wind_y_ref[...], below[4:6]], axis=0)
        next_y = jnp.concatenate([above[7:8], wind_y_ref[...], below[4:7]], axis=0)
        gain_x, loss_x = jnp.maximum(wind_x, 0.0), jnp.minimum(wind_x, 0.0)
        gain_y, loss_y = jnp.maximum(wind_y, 0.0), jnp.minimum(wind_y, 0.0)
        keep = 1.0 + loss_x - pltpu.roll(gain_x, 127, 1) + loss_y - jnp.maximum(next_y, 0.0)
        parts = [
            keep, gain_x, -pltpu.roll(loss_x, 127, 1), gain_y, -jnp.minimum(next_y, 0.0)
        ]
        for k, part in enumerate(parts):
            for w in range(8):
                coef_ref[k * 8 + w] = jnp.broadcast_to(part[w : w + 1], (PIECE, 128))

    fetch(block).wait()
    slot = block % 2
    for piece in range(count // PIECE):
        at = piece * PIECE
        field = (
            [ref[at : at + PIECE].astype(jnp.float32) for ref in (a0, a1, a2)]
            + [fetched_ref[slot, pl.ds(4 * at + r, PIECE, 4), :] for r in range(4)]
            + [ref[at : at + PIECE].astype(jnp.float32) for ref in (b0, b1, b2)]
        )
        for step in range(STEPS):
            new = []
            for i in range(len(field) - 2):
                w = step + i
                here = field[i + 1]
                new.append(
                    coef_ref[w] * here
                    + coef_ref[8 + w] * pltpu.roll(here, 1, 1)
                    + coef_ref[16 + w] * pltpu.roll(here, 127, 1)
                    + coef_ref[24 + w] * field[i]
                    + coef_ref[32 + w] * field[i + 2]
                )
            field = new
        for r in range(4):
            out_ref[at : at + PIECE, r * 128 : (r + 1) * 128] = field[r].astype(jnp.bfloat16)


def transport(pulses, above, below, wind_x, wind_y, span, into=None, block=128):
    tracers = pulses.shape[0] // 4
    start, size = span
    skip, steps = start // block, size // block
    halo = [
        pl.BlockSpec((block, 128), lambda i, r=r: (r * steps + i, 0)) for r in range(STEPS)
    ]
    last = [pl.BlockSpec((16, 128), lambda i: (STEPS * size // 16, 0))] * 2
    wind = pl.BlockSpec((4, 128), lambda i: (0, 0))
    operands = [pulses, *[above] * 3, *[below] * 3, above, below, wind_x, wind_y]
    specs = [pl.BlockSpec(memory_space=pltpu.HBM)] + halo + halo + last
    specs += [wind, wind]
    aliases = {}
    if into is not None:
        aliases = {len(operands): 0}
        operands.append(into)
        specs.append(pl.BlockSpec(memory_space=pl.ANY))
    return pl.pallas_call(
        functools.partial(transport_body, skip),
        grid=(steps,),
        in_specs=specs,
        out_specs=pl.BlockSpec((block, 512), lambda i: (skip + i, 0)),
        out_shape=jax.ShapeDtypeStruct((tracers, 512), jnp.bfloat16),
        scratch_shapes=[
            pltpu.VMEM((40, PIECE, 128), jnp.float32),
            pltpu.VMEM((2, 4 * block, 128), jnp.float32),
            pltpu.SemaphoreType.DMA((2,)),
        ],
        input_output_aliases=aliases,
        compiler_params=pltpu.CompilerParams(vmem_limit_bytes=GRANT),
        name="transport",
    )(*operands)


def jacobian_body(rows_ref, low_ref, high_ref, out_ref, full_ref):
    @pl.when(pl.program_id(0) == 0)
    def _():
        count, width = rows_ref.shape
        mine = rows_ref[...].astype(jnp.float32).reshape(count // 8, 8, width)
        swap = pltpu.roll(mine, 4, 1)
        top = lax.broadcasted_iota(jnp.int32, mine.shape, 1) < 4
        left = jnp.where(top, mine, swap).reshape(count, width)
        right = jnp.where(top, swap, mine).reshape(count, width)
        full_ref[:, :width] = left.astype(jnp.bfloat16)
        full_ref[:, width:] = right.astype(jnp.bfloat16)

    dims = (((1,), (1,)), ((), ()))
    full = full_ref[...]
    low = lax.dot_general(full, low_ref[...], dims, preferred_element_type=jnp.float32)
    high = lax.dot_general(full, high_ref[...], dims, preferred_element_type=jnp.float32)
    row = lax.broadcasted_iota(jnp.int32, low.shape, 0)
    out_ref[...] = jnp.where((row & 4) == 0, low, high).astype(jnp.bfloat16)


def jacobian(rows, sampled, block=256):
    tracers = sampled.shape[0]
    count, width = rows.shape
    steps = tracers // 2 // block
    return pl.pallas_call(
        jacobian_body,
        grid=(steps,),
        in_specs=[
            pl.BlockSpec((count, width), lambda i: (0, 0)),
            pl.BlockSpec((block, 512), lambda i: (i, 0)),
            pl.BlockSpec((block, 512), lambda i: (steps + i, 0)),
        ],
        out_specs=pl.BlockSpec((count, block), lambda i: (0, i)),
        out_shape=jax.ShapeDtypeStruct((count, tracers // 2), jnp.bfloat16),
        scratch_shapes=[pltpu.VMEM((count, 2 * width), jnp.bfloat16)],
        compiler_params=pltpu.CompilerParams(vmem_limit_bytes=GRANT),
        name="jacobian",
    )(rows, sampled, sampled)


def gram_body(apart, place_ref, same_ref, cross_ref, across_ref, other_ref, *refs):
    cols, outs, scratch = refs[:8], refs[8:-3], refs[-3:]
    rows_ref, cols_ref, sum_ref = scratch
    block = same_ref.shape[0]
    parts = [same_ref[...], cross_ref[...]]
    for ref in (across_ref, other_ref):
        parts += [ref[s : s + block] for s in range(0, ref.shape[0], block)]
    for k, part in enumerate(parts):
        at = pl.multiple_of(place_ref[k] * block, block)
        rows_ref[:, pl.ds(at, block)] = part.T
    for k, ref in enumerate(cols):
        at = pl.multiple_of(place_ref[8 + k] * block, block)
        cols_ref[pl.ds(at, block), :] = ref[...]
    tile = lax.dot_general(
        rows_ref[...], cols_ref[...], (((1,), (0,)), ((), ())), preferred_element_type=jnp.float32
    )
    if not apart:
        outs[0][...] = tile.astype(jnp.bfloat16)
        return
    sum_ref[...] = tile
    deep = len(outs)
    size = tile.shape[0] // deep
    for d, out_ref in enumerate(outs):
        at = pl.multiple_of(((place_ref[16] + d) % deep) * size, size)
        out_ref[...] = sum_ref[pl.ds(at, size), :].astype(out_ref.dtype)


def gram_tile(place, same, cross, across, other, cols, apart):
    obs, width = cols[0].shape
    rows = same.shape[1]
    if apart:
        size = (rows // apart, width)
        shapes = [jax.ShapeDtypeStruct(size, jnp.float32)]
        shapes += [jax.ShapeDtypeStruct(size, jnp.bfloat16)] * (apart - 1)
    else:
        shapes = [jax.ShapeDtypeStruct((rows, width), jnp.bfloat16)]
    whole = pl.BlockSpec(memory_space=pltpu.VMEM)
    return pl.pallas_call(
        functools.partial(gram_body, apart),
        in_specs=[pl.BlockSpec(memory_space=pltpu.SMEM)] + [whole] * (4 + len(cols)),
        out_specs=[whole] * len(shapes),
        out_shape=shapes,
        scratch_shapes=[
            pltpu.VMEM((rows, len(cols) * obs), jnp.bfloat16),
            pltpu.VMEM((len(cols) * obs, width), jnp.bfloat16),
            pltpu.VMEM((rows, width), jnp.float32),
        ],
        compiler_params=pltpu.CompilerParams(vmem_limit_bytes=GRANT),
        name="gram",
    )(place, same, cross, across, other, *cols)


def on_device(pulses, wind_x, wind_y, obs_tile, obs_weight, obs_precision):
    tracers = pulses.shape[0]
    cells = lax.axis_size(CELLS)
    obs = obs_tile.shape[0]
    half = tracers // 2
    pulses = pulses.reshape(tracers * 4, 128)

    messages = edges(pulses, wind_x, wind_y)
    halos = []
    for k in range(2):
        halos.append((shifted(messages[2 * k + 1], CELLS, 1), shifted(messages[2 * k], CELLS, -1)))
    sampled = None
    pulses = pltpu.with_memory_space_constraint(pulses, pltpu.HBM)
    for span, (above, below) in zip(spans(tracers), halos):
        sampled = transport(pulses, above, below, wind_x, wind_y, span, sampled)

    tile = obs_tile[:, 0]
    order = jnp.arange(obs)
    earlier = (tile[:, None] == tile[None, :]) & (order[None, :] < order[:, None])
    slot = 2 * CAP * tile + jnp.sum(earlier.astype(jnp.int32), axis=1)
    lanes = jnp.arange(2 * CAP * cells)[None, :]
    chosen = [(slot[:, None] + CAP * h == lanes).astype(jnp.bfloat16) for h in range(2)]
    wide = obs_weight.astype(jnp.float32)
    averaging = (wide / jnp.sum(wide, axis=1, keepdims=True)).astype(jnp.bfloat16)
    split = obs_weight.shape[1] // 2
    rows_out = lax.dot_general(
        jnp.concatenate(chosen, axis=0),
        jnp.concatenate([averaging[:, :split], averaging[:, split:]], axis=0),
        (((0,), (0,)), ((), ())),
        preferred_element_type=jnp.float32,
    ).astype(jnp.bfloat16)
    rows_in = exchanged(rows_out.reshape(cells, 2 * CAP, split), CELLS)

    jac_tile = jacobian(rows_in.reshape(cells * 2 * CAP, split), sampled)
    jac_back = exchanged(jac_tile.reshape(cells, 2 * CAP, half), CELLS)
    jac_back = jac_back.reshape(cells * 2 * CAP, half)
    jac = [
        lax.dot_general(
            c, jac_back, (((1,), (0,)), ((), ())), preferred_element_type=jnp.float32
        )
        for c in chosen
    ]
    precision = obs_precision.astype(jnp.float32)[:, None]
    weighted = [(precision * j).astype(jnp.bfloat16) for j in jac]
    low, high = [j.astype(jnp.bfloat16) for j in jac]

    group = lax.axis_size(XY)
    peers = lax.axis_size(TRACERS)
    here = lax.axis_index(XY)
    odd = here % 2
    pairs = [(i // peers, i % peers) for i in range(group * peers)]
    to_same = [(a * peers + q, (2 * q + a % 2) * peers + a // 2) for a, q in pairs]
    to_cross = [(a * peers + q, (2 * q + 1 - a % 2) * peers + a // 2) for a, q in pairs]
    same = lax.ppermute(jnp.where(odd == 0, low, high), PLANE, to_same)
    cross = lax.ppermute(jnp.where(odd == 0, high, low), PLANE, to_cross)
    across = shifted(jnp.concatenate([same, cross], axis=0), "xh", 1)
    other = shifted(jnp.concatenate([same, cross, across], axis=0), "core", 1)

    deep = lax.axis_size("y")
    cols = []
    for part, value in enumerate(weighted):
        beside = shifted(value, "xl", 1)
        cols.append([value, beside])
        for source in (value, beside):
            for d in range(1, deep):
                cols[part].append(shifted(source, "y", d))
    xl, y = lax.axis_index("xl"), lax.axis_index("y")
    owners = [here, (1 - xl) * deep + y]
    owners += [xl * deep + (y - d) % deep for d in range(1, deep)]
    owners += [(1 - xl) * deep + (y - d) % deep for d in range(1, deep)]
    tracer = lax.axis_index(TRACERS)
    row_owners = [2 * (tracer ^ flip) + (odd ^ s) for flip in (0, 2, 1, 3) for s in (0, 1)]
    place = jnp.stack(row_owners + owners + [lax.axis_index("z")]).astype(jnp.int32)

    depth = lax.axis_size("z")
    tile = gram_tile(place, same, cross, across, other, cols[0], 0)[0]
    parts = exchanged(tile.reshape(depth, half // depth, half), "z")
    total = jnp.sum(parts.astype(jnp.float32), axis=0)
    blocks = gram_tile(place, same, cross, across, other, cols[1], depth)
    last = blocks[0]
    for d in (4, 3, 5, 2, 6, 1, 7):
        last = last + shifted(blocks[d], "z", d).astype(jnp.float32)
    return jnp.concatenate([total, last], axis=1)


def solution(mesh):
    fine = Mesh(mesh.devices.reshape(2, 4, 8, 2, 2), CELLS + TRACERS)
    placed = (
        P(TRACERS, CELLS, None),
        P(CELLS, None),
        P(CELLS, None),
        P(CELLS, None),
        P(CELLS, None),
        P(CELLS),
    )
    return jax.shard_map(
        on_device, mesh=fine, in_specs=placed, out_specs=P(CELLS, TRACERS), check_vma=False
    )
```

```python
import functools

import jax
import jax.numpy as jnp
from jax import lax
from jax.experimental import pallas as pl
from jax.experimental.pallas import tpu as pltpu
from jax.sharding import Mesh, PartitionSpec as P


STEPS = 3
GRANT = 16 * 1024 * 1024
CAP = 4
XY = ("xl", "y")
CELLS = ("xl", "y", "z")
TRACERS = ("xh", "core")
PLANE = XY + TRACERS


def shifted(value, axis, steps):
    count = lax.axis_size(axis)
    return lax.ppermute(value, axis, [(i, (i + steps) % count) for i in range(count)])


def exchanged(value, axis):
    return lax.all_to_all(value, axis, split_axis=0, concat_axis=0, tiled=True)


def edge_rows(pulse_ref, wind_x_ref, wind_y_ref, *out_refs):
    tracers = pulse_ref.shape[0] // 4
    rows = [pulse_ref[pl.ds(r, tracers, 4), :].astype(jnp.bfloat16) for r in range(4)]
    winds = jnp.concatenate([wind_x_ref[...], wind_y_ref[...]], axis=0)
    coarse = winds.astype(jnp.bfloat16).astype(jnp.float32)
    both = jnp.concatenate([coarse, winds - coarse], axis=0).astype(jnp.bfloat16)
    for k, (start, size) in enumerate(spans(tracers)):
        for edge in range(2):
            ref = out_refs[2 * k + edge]
            for r in range(STEPS):
                ref[r * size : (r + 1) * size] = rows[r + edge][start : start + size]
            ref[STEPS * size :] = both


def spans(tracers):
    cut = tracers * 5 // 8
    return [(0, cut), (cut, tracers - cut)]


def edges(pulses, wind_x, wind_y):
    tracers = pulses.shape[0] // 4
    shapes = []
    for start, size in spans(tracers):
        shapes += [jax.ShapeDtypeStruct((STEPS * size + 16, 128), jnp.bfloat16)] * 2
    return pl.pallas_call(edge_rows, out_shape=shapes, name="edges")(pulses, wind_x, wind_y)


PIECE = 16


def transport_body(
    skip, pulse_ref, a0, a1, a2, b0, b1, b2, a_winds, b_winds, wind_x_ref, wind_y_ref, *refs
):
    out_ref, coef_ref, fetched_ref, sems = refs[-4:]
    count = out_ref.shape[0]
    block = pl.program_id(0)

    def fetch(i):
        source = pulse_ref.at[pl.ds((skip + i) * 4 * count, 4 * count)]
        return pltpu.make_async_copy(source, fetched_ref.at[i % 2], sems.at[i % 2])

    @pl.when(block == 0)
    def _():
        fetch(block).start()

    @pl.when(block + 1 < pl.num_programs(0))
    def _():
        fetch(block + 1).start()

    @pl.when(pl.program_id(0) == 0)
    def _():
        above = a_winds[...].astype(jnp.float32)
        below = b_winds[...].astype(jnp.float32)
        above = above[0:8] + above[8:16]
        below = below[0:8] + below[8:16]
        wind_x = jnp.concatenate([above[2:4], wind_x_ref[...], below[0:2]], axis=0)
        wind_y = jnp.concatenate([above[6:8], wind_y_ref[...], below[4:6]], axis=0)
        next_y = jnp.concatenate([above[7:8], wind_y_ref[...], below[4:7]], axis=0)
        gain_x, loss_x = jnp.maximum(wind_x, 0.0), jnp.minimum(wind_x, 0.0)
        gain_y, loss_y = jnp.maximum(wind_y, 0.0), jnp.minimum(wind_y, 0.0)
        keep = 1.0 + loss_x - pltpu.roll(gain_x, 127, 1) + loss_y - jnp.maximum(next_y, 0.0)
        parts = [
            keep, gain_x, -pltpu.roll(loss_x, 127, 1), gain_y, -jnp.minimum(next_y, 0.0)
        ]
        for k, part in enumerate(parts):
            for w in range(8):
                coef_ref[k * 8 + w] = jnp.broadcast_to(part[w : w + 1], (PIECE, 128))

    fetch(block).wait()
    slot = block % 2
    for piece in range(count // PIECE):
        at = piece * PIECE
        field = (
            [ref[at : at + PIECE].astype(jnp.float32) for ref in (a0, a1, a2)]
            + [fetched_ref[slot, pl.ds(4 * at + r, PIECE, 4), :] for r in range(4)]
            + [ref[at : at + PIECE].astype(jnp.float32) for ref in (b0, b1, b2)]
        )
        for step in range(STEPS):
            new = []
            for i in range(len(field) - 2):
                w = step + i
                here = field[i + 1]
                new.append(
                    coef_ref[w] * here
                    + coef_ref[8 + w] * pltpu.roll(here, 1, 1)
                    + coef_ref[16 + w] * pltpu.roll(here, 127, 1)
                    + coef_ref[24 + w] * field[i]
                    + coef_ref[32 + w] * field[i + 2]
                )
            field = new
        for r in range(4):
            out_ref[at : at + PIECE, r * 128 : (r + 1) * 128] = field[r].astype(jnp.bfloat16)


def transport(pulses, above, below, wind_x, wind_y, span, into=None, block=128):
    tracers = pulses.shape[0] // 4
    start, size = span
    skip, steps = start // block, size // block
    halo = [
        pl.BlockSpec((block, 128), lambda i, r=r: (r * steps + i, 0)) for r in range(STEPS)
    ]
    last = [pl.BlockSpec((16, 128), lambda i: (STEPS * size // 16, 0))] * 2
    wind = pl.BlockSpec((4, 128), lambda i: (0, 0))
    operands = [pulses, *[above] * 3, *[below] * 3, above, below, wind_x, wind_y]
    specs = [pl.BlockSpec(memory_space=pltpu.HBM)] + halo + halo + last
    specs += [wind, wind]
    aliases = {}
    if into is not None:
        aliases = {len(operands): 0}
        operands.append(into)
        specs.append(pl.BlockSpec(memory_space=pl.ANY))
    return pl.pallas_call(
        functools.partial(transport_body, skip),
        grid=(steps,),
        in_specs=specs,
        out_specs=pl.BlockSpec((block, 512), lambda i: (skip + i, 0)),
        out_shape=jax.ShapeDtypeStruct((tracers, 512), jnp.bfloat16),
        scratch_shapes=[
            pltpu.VMEM((40, PIECE, 128), jnp.float32),
            pltpu.VMEM((2, 4 * block, 128), jnp.float32),
            pltpu.SemaphoreType.DMA((2,)),
        ],
        input_output_aliases=aliases,
        compiler_params=pltpu.CompilerParams(vmem_limit_bytes=GRANT),
        name="transport",
    )(*operands)


def jacobian_body(rows_ref, low_ref, high_ref, out_ref, full_ref):
    @pl.when(pl.program_id(0) == 0)
    def _():
        count, width = rows_ref.shape
        mine = rows_ref[...].astype(jnp.float32).reshape(count // 8, 8, width)
        swap = pltpu.roll(mine, 4, 1)
        top = lax.broadcasted_iota(jnp.int32, mine.shape, 1) < 4
        left = jnp.where(top, mine, swap).reshape(count, width)
        right = jnp.where(top, swap, mine).reshape(count, width)
        full_ref[:, :width] = left.astype(jnp.bfloat16)
        full_ref[:, width:] = right.astype(jnp.bfloat16)

    dims = (((1,), (1,)), ((), ()))
    full = full_ref[...]
    low = lax.dot_general(full, low_ref[...], dims, preferred_element_type=jnp.float32)
    high = lax.dot_general(full, high_ref[...], dims, preferred_element_type=jnp.float32)
    row = lax.broadcasted_iota(jnp.int32, low.shape, 0)
    out_ref[...] = jnp.where((row & 4) == 0, low, high).astype(jnp.bfloat16)


def jacobian(rows, sampled, block=256):
    tracers = sampled.shape[0]
    count, width = rows.shape
    steps = tracers // 2 // block
    return pl.pallas_call(
        jacobian_body,
        grid=(steps,),
        in_specs=[
            pl.BlockSpec((count, width), lambda i: (0, 0)),
            pl.BlockSpec((block, 512), lambda i: (i, 0)),
            pl.BlockSpec((block, 512), lambda i: (steps + i, 0)),
        ],
        out_specs=pl.BlockSpec((count, block), lambda i: (0, i)),
        out_shape=jax.ShapeDtypeStruct((count, tracers // 2), jnp.bfloat16),
        scratch_shapes=[pltpu.VMEM((count, 2 * width), jnp.bfloat16)],
        compiler_params=pltpu.CompilerParams(vmem_limit_bytes=GRANT),
        name="jacobian",
    )(rows, sampled, sampled)


def gram_body(apart, place_ref, *refs):
    rows, cols, outs, scratch = refs[:8], refs[8:16], refs[16:-3], refs[-3:]
    rows_ref, cols_ref, sum_ref = scratch
    block = rows[0].shape[0]
    for k, ref in enumerate(rows):
        at = pl.multiple_of(place_ref[k] * block, block)
        rows_ref[:, pl.ds(at, block)] = ref[...].T
    for k, ref in enumerate(cols):
        at = pl.multiple_of(place_ref[8 + k] * block, block)
        cols_ref[pl.ds(at, block), :] = ref[...]
    tile = lax.dot_general(
        rows_ref[...], cols_ref[...], (((1,), (0,)), ((), ())), preferred_element_type=jnp.float32
    )
    if not apart:
        outs[0][...] = tile.astype(jnp.bfloat16)
        return
    sum_ref[...] = tile
    deep = len(outs)
    size = tile.shape[0] // deep
    for d, out_ref in enumerate(outs):
        at = pl.multiple_of(((place_ref[16] + d) % deep) * size, size)
        out_ref[...] = sum_ref[pl.ds(at, size), :].astype(out_ref.dtype)


def gram_tile(place, pieces, cols, apart):
    obs, width = cols[0].shape
    rows = pieces[0].shape[1]
    if apart:
        size = (rows // apart, width)
        shapes = [jax.ShapeDtypeStruct(size, jnp.float32)]
        shapes += [jax.ShapeDtypeStruct(size, jnp.bfloat16)] * (apart - 1)
    else:
        shapes = [jax.ShapeDtypeStruct((rows, width), jnp.bfloat16)]
    whole = pl.BlockSpec(memory_space=pltpu.VMEM)
    return pl.pallas_call(
        functools.partial(gram_body, apart),
        in_specs=[pl.BlockSpec(memory_space=pltpu.SMEM)] + [whole] * (len(pieces) + len(cols)),
        out_specs=[whole] * len(shapes),
        out_shape=shapes,
        scratch_shapes=[
            pltpu.VMEM((rows, len(cols) * obs), jnp.bfloat16),
            pltpu.VMEM((len(cols) * obs, width), jnp.bfloat16),
            pltpu.VMEM((rows, width), jnp.float32),
        ],
        compiler_params=pltpu.CompilerParams(vmem_limit_bytes=GRANT),
        name="gram",
    )(place, *pieces, *cols)


def on_device(pulses, wind_x, wind_y, obs_tile, obs_weight, obs_precision):
    tracers = pulses.shape[0]
    cells = lax.axis_size(CELLS)
    obs = obs_tile.shape[0]
    half = tracers // 2
    pulses = pulses.reshape(tracers * 4, 128)

    messages = edges(pulses, wind_x, wind_y)
    halos = []
    for k in range(2):
        halos.append((shifted(messages[2 * k + 1], CELLS, 1), shifted(messages[2 * k], CELLS, -1)))
    sampled = None
    pulses = pltpu.with_memory_space_constraint(pulses, pltpu.HBM)
    for span, (above, below) in zip(spans(tracers), halos):
        sampled = transport(pulses, above, below, wind_x, wind_y, span, sampled)

    tile = obs_tile[:, 0]
    order = jnp.arange(obs)
    earlier = (tile[:, None] == tile[None, :]) & (order[None, :] < order[:, None])
    slot = 2 * CAP * tile + jnp.sum(earlier.astype(jnp.int32), axis=1)
    lanes = jnp.arange(2 * CAP * cells)[None, :]
    chosen = [(slot[:, None] + CAP * h == lanes).astype(jnp.bfloat16) for h in range(2)]
    wide = obs_weight.astype(jnp.float32)
    averaging = (wide / jnp.sum(wide, axis=1, keepdims=True)).astype(jnp.bfloat16)
    split = obs_weight.shape[1] // 2
    rows_out = lax.dot_general(
        jnp.concatenate(chosen, axis=0),
        jnp.concatenate([averaging[:, :split], averaging[:, split:]], axis=0),
        (((0,), (0,)), ((), ())),
        preferred_element_type=jnp.float32,
    ).astype(jnp.bfloat16)
    rows_in = exchanged(rows_out.reshape(cells, 2 * CAP, split), CELLS)

    jac_tile = jacobian(rows_in.reshape(cells * 2 * CAP, split), sampled)
    jac_back = exchanged(jac_tile.reshape(cells, 2 * CAP, half), CELLS)
    jac_back = jac_back.reshape(cells * 2 * CAP, half)
    jac = [
        lax.dot_general(
            c, jac_back, (((1,), (0,)), ((), ())), preferred_element_type=jnp.float32
        )
        for c in chosen
    ]
    precision = obs_precision.astype(jnp.float32)[:, None]
    weighted = [(precision * j).astype(jnp.bfloat16) for j in jac]
    low, high = [j.astype(jnp.bfloat16) for j in jac]

    group = lax.axis_size(XY)
    peers = lax.axis_size(TRACERS)
    here = lax.axis_index(XY)
    odd = here % 2
    pairs = [(i // peers, i % peers) for i in range(group * peers)]
    mine = jnp.where(odd == 0, low, high), jnp.where(odd == 0, high, low)
    pieces = []
    for flip in (0, 2):
        for s, value in enumerate(mine):
            path = [
                (a * peers + q, (2 * q + (a % 2 ^ s)) * peers + (a // 2 ^ flip)) for a, q in pairs
            ]
            pieces.append(lax.ppermute(value, PLANE, path))
    for k in range(4):
        pieces.append(shifted(pieces[k], "core", 1))

    deep = lax.axis_size("y")
    cols = []
    for part, value in enumerate(weighted):
        beside = shifted(value, "xl", 1)
        cols.append([value, beside])
        for d in range(1, deep):
            cols[part].append(shifted(value, "y", d))
        for d in range(1, deep):
            if part == 0:
                cols[part].append(shifted(beside, "y", d))
            else:
                path = [(k, (1 - k // deep) * deep + (k + d) % deep) for k in range(group)]
                cols[part].append(lax.ppermute(value, XY, path))
    xl, y = lax.axis_index("xl"), lax.axis_index("y")
    owners = [here, (1 - xl) * deep + y]
    owners += [xl * deep + (y - d) % deep for d in range(1, deep)]
    owners += [(1 - xl) * deep + (y - d) % deep for d in range(1, deep)]
    tracer = lax.axis_index(TRACERS)
    row_owners = [2 * (tracer ^ flip) + (odd ^ s) for flip in (0, 2, 1, 3) for s in (0, 1)]
    place = jnp.stack(row_owners + owners + [lax.axis_index("z")]).astype(jnp.int32)

    depth = lax.axis_size("z")
    tile = gram_tile(place, pieces, cols[0], 0)[0]
    parts = exchanged(tile.reshape(depth, half // depth, half), "z")
    total = jnp.sum(parts.astype(jnp.float32), axis=0)
    blocks = gram_tile(place, pieces, cols[1], depth)
    last = blocks[0]
    for d in (4, 3, 5, 2, 6, 1, 7):
        last = last + shifted(blocks[d], "z", d).astype(jnp.float32)
    return jnp.concatenate([total, last], axis=1)


def solution(mesh):
    fine = Mesh(mesh.devices.reshape(2, 4, 8, 2, 2), CELLS + TRACERS)
    placed = (
        P(TRACERS, CELLS, None),
        P(CELLS, None),
        P(CELLS, None),
        P(CELLS, None),
        P(CELLS, None),
        P(CELLS),
    )
    return jax.shard_map(
        on_device, mesh=fine, in_specs=placed, out_specs=P(CELLS, TRACERS), check_vma=False
    )
```

```python
import functools

import jax
import jax.numpy as jnp
from jax import lax
from jax.experimental import pallas as pl
from jax.experimental.pallas import tpu as pltpu
from jax.sharding import Mesh, PartitionSpec as P


STEPS = 3
GRANT = 16 * 1024 * 1024
CAP = 4
XY = ("xl", "y")
CELLS = ("xl", "y", "z")
TRACERS = ("xh", "core")
PLANE = XY + TRACERS


def shifted(value, axis, steps):
    count = lax.axis_size(axis)
    return lax.ppermute(value, axis, [(i, (i + steps) % count) for i in range(count)])


def exchanged(value, axis):
    return lax.all_to_all(value, axis, split_axis=0, concat_axis=0, tiled=True)


def edge_rows(pulse_ref, wind_x_ref, wind_y_ref, *out_refs):
    tracers = pulse_ref.shape[0] // 4
    rows = [pulse_ref[pl.ds(r, tracers, 4), :].astype(jnp.bfloat16) for r in range(4)]
    winds = jnp.concatenate([wind_x_ref[...], wind_y_ref[...]], axis=0)
    coarse = winds.astype(jnp.bfloat16).astype(jnp.float32)
    both = jnp.concatenate([coarse, winds - coarse], axis=0).astype(jnp.bfloat16)
    for k, (start, size) in enumerate(spans(tracers)):
        for edge in range(2):
            ref = out_refs[2 * k + edge]
            for r in range(STEPS):
                ref[r * size : (r + 1) * size] = rows[r + edge][start : start + size]
            ref[STEPS * size :] = both


def spans(tracers):
    cut = tracers * 5 // 8
    return [(0, cut), (cut, tracers - cut)]


def edges(pulses, wind_x, wind_y):
    tracers = pulses.shape[0] // 4
    shapes = []
    for start, size in spans(tracers):
        shapes += [jax.ShapeDtypeStruct((STEPS * size + 16, 128), jnp.bfloat16)] * 2
    return pl.pallas_call(edge_rows, out_shape=shapes, name="edges")(pulses, wind_x, wind_y)


PIECE = 16


def transport_body(
    skip, pulse_ref, a0, a1, a2, b0, b1, b2, a_winds, b_winds, wind_x_ref, wind_y_ref, *refs
):
    out_ref, coef_ref, fetched_ref, sems = refs[-4:]
    count = out_ref.shape[0]
    block = pl.program_id(0)

    def fetch(i):
        source = pulse_ref.at[pl.ds((skip + i) * 4 * count, 4 * count)]
        return pltpu.make_async_copy(source, fetched_ref.at[i % 2], sems.at[i % 2])

    @pl.when(block == 0)
    def _():
        fetch(block).start()

    @pl.when(block + 1 < pl.num_programs(0))
    def _():
        fetch(block + 1).start()

    @pl.when(pl.program_id(0) == 0)
    def _():
        above = a_winds[...].astype(jnp.float32)
        below = b_winds[...].astype(jnp.float32)
        above = above[0:8] + above[8:16]
        below = below[0:8] + below[8:16]
        wind_x = jnp.concatenate([above[2:4], wind_x_ref[...], below[0:2]], axis=0)
        wind_y = jnp.concatenate([above[6:8], wind_y_ref[...], below[4:6]], axis=0)
        next_y = jnp.concatenate([above[7:8], wind_y_ref[...], below[4:7]], axis=0)
        gain_x, loss_x = jnp.maximum(wind_x, 0.0), jnp.minimum(wind_x, 0.0)
        gain_y, loss_y = jnp.maximum(wind_y, 0.0), jnp.minimum(wind_y, 0.0)
        keep = 1.0 + loss_x - pltpu.roll(gain_x, 127, 1) + loss_y - jnp.maximum(next_y, 0.0)
        parts = [
            keep, gain_x, -pltpu.roll(loss_x, 127, 1), gain_y, -jnp.minimum(next_y, 0.0)
        ]
        for k, part in enumerate(parts):
            for w in range(8):
                coef_ref[k * 8 + w] = jnp.broadcast_to(part[w : w + 1], (PIECE, 128))

    fetch(block).wait()
    slot = block % 2
    for piece in range(count // PIECE):
        at = piece * PIECE
        field = (
            [ref[at : at + PIECE].astype(jnp.float32) for ref in (a0, a1, a2)]
            + [fetched_ref[slot, pl.ds(4 * at + r, PIECE, 4), :] for r in range(4)]
            + [ref[at : at + PIECE].astype(jnp.float32) for ref in (b0, b1, b2)]
        )
        for step in range(STEPS):
            new = []
            for i in range(len(field) - 2):
                w = step + i
                here = field[i + 1]
                new.append(
                    coef_ref[w] * here
                    + coef_ref[8 + w] * pltpu.roll(here, 1, 1)
                    + coef_ref[16 + w] * pltpu.roll(here, 127, 1)
                    + coef_ref[24 + w] * field[i]
                    + coef_ref[32 + w] * field[i + 2]
                )
            field = new
        for r in range(4):
            out_ref[at : at + PIECE, r * 128 : (r + 1) * 128] = field[r].astype(jnp.bfloat16)


def transport(pulses, above, below, wind_x, wind_y, span, into=None, block=128):
    tracers = pulses.shape[0] // 4
    start, size = span
    skip, steps = start // block, size // block
    halo = [
        pl.BlockSpec((block, 128), lambda i, r=r: (r * steps + i, 0)) for r in range(STEPS)
    ]
    last = [pl.BlockSpec((16, 128), lambda i: (STEPS * size // 16, 0))] * 2
    wind = pl.BlockSpec((4, 128), lambda i: (0, 0))
    operands = [pulses, *[above] * 3, *[below] * 3, above, below, wind_x, wind_y]
    specs = [pl.BlockSpec(memory_space=pltpu.HBM)] + halo + halo + last
    specs += [wind, wind]
    aliases = {}
    if into is not None:
        aliases = {len(operands): 0}
        operands.append(into)
        specs.append(pl.BlockSpec(memory_space=pl.ANY))
    return pl.pallas_call(
        functools.partial(transport_body, skip),
        grid=(steps,),
        in_specs=specs,
        out_specs=pl.BlockSpec((block, 512), lambda i: (skip + i, 0)),
        out_shape=jax.ShapeDtypeStruct((tracers, 512), jnp.bfloat16),
        scratch_shapes=[
            pltpu.VMEM((40, PIECE, 128), jnp.float32),
            pltpu.VMEM((2, 4 * block, 128), jnp.float32),
            pltpu.SemaphoreType.DMA((2,)),
        ],
        input_output_aliases=aliases,
        compiler_params=pltpu.CompilerParams(vmem_limit_bytes=GRANT),
        name="transport",
    )(*operands)


def jacobian_body(rows_ref, low_ref, high_ref, out_ref, full_ref):
    @pl.when(pl.program_id(0) == 0)
    def _():
        count, width = rows_ref.shape
        mine = rows_ref[...].astype(jnp.float32).reshape(count // 8, 8, width)
        swap = pltpu.roll(mine, 4, 1)
        top = lax.broadcasted_iota(jnp.int32, mine.shape, 1) < 4
        left = jnp.where(top, mine, swap).reshape(count, width)
        right = jnp.where(top, swap, mine).reshape(count, width)
        full_ref[:, :width] = left.astype(jnp.bfloat16)
        full_ref[:, width:] = right.astype(jnp.bfloat16)

    dims = (((1,), (1,)), ((), ()))
    full = full_ref[...]
    low = lax.dot_general(full, low_ref[...], dims, preferred_element_type=jnp.float32)
    high = lax.dot_general(full, high_ref[...], dims, preferred_element_type=jnp.float32)
    row = lax.broadcasted_iota(jnp.int32, low.shape, 0)
    out_ref[...] = jnp.where((row & 4) == 0, low, high).astype(jnp.bfloat16)


def jacobian(rows, sampled, block=256):
    tracers = sampled.shape[0]
    count, width = rows.shape
    steps = tracers // 2 // block
    return pl.pallas_call(
        jacobian_body,
        grid=(steps,),
        in_specs=[
            pl.BlockSpec((count, width), lambda i: (0, 0)),
            pl.BlockSpec((block, 512), lambda i: (i, 0)),
            pl.BlockSpec((block, 512), lambda i: (steps + i, 0)),
        ],
        out_specs=pl.BlockSpec((count, block), lambda i: (0, i)),
        out_shape=jax.ShapeDtypeStruct((count, tracers // 2), jnp.bfloat16),
        scratch_shapes=[pltpu.VMEM((count, 2 * width), jnp.bfloat16)],
        compiler_params=pltpu.CompilerParams(vmem_limit_bytes=GRANT),
        name="jacobian",
    )(rows, sampled, sampled)


def gram_body(apart, place_ref, *refs):
    outs = apart if apart else 1
    rows, cols, outs, scratch = refs[:8], refs[8 : -3 - outs], refs[-3 - outs : -3], refs[-3:]
    rows_ref, cols_ref, sum_ref = scratch
    block = rows[0].shape[0]
    for k, ref in enumerate(rows):
        at = pl.multiple_of(place_ref[k] * block, block)
        rows_ref[:, pl.ds(at, block)] = ref[...].T
    if len(cols) > 1:
        for k, ref in enumerate(cols):
            at = pl.multiple_of(place_ref[8 + k] * block, block)
            cols_ref[pl.ds(at, block), :] = ref[...]
        right = cols_ref[...]
    else:
        right = cols[0][...]
    tile = lax.dot_general(
        rows_ref[...], right, (((1,), (0,)), ((), ())), preferred_element_type=jnp.float32
    )
    if not apart:
        outs[0][...] = tile.astype(jnp.bfloat16)
        return
    sum_ref[...] = tile
    deep = len(outs)
    size = tile.shape[0] // deep
    for d, out_ref in enumerate(outs):
        at = pl.multiple_of(((place_ref[16] + d) % deep) * size, size)
        out_ref[...] = sum_ref[pl.ds(at, size), :].astype(out_ref.dtype)


def gram_tile(place, pieces, cols, apart):
    count, width = sum(v.shape[0] for v in cols), cols[0].shape[1]
    rows = pieces[0].shape[1]
    if apart:
        size = (rows // apart, width)
        shapes = [jax.ShapeDtypeStruct(size, jnp.float32)]
        shapes += [jax.ShapeDtypeStruct(size, jnp.bfloat16)] * (apart - 1)
    else:
        shapes = [jax.ShapeDtypeStruct((rows, width), jnp.bfloat16)]
    whole = pl.BlockSpec(memory_space=pltpu.VMEM)
    return pl.pallas_call(
        functools.partial(gram_body, apart),
        in_specs=[pl.BlockSpec(memory_space=pltpu.SMEM)] + [whole] * (len(pieces) + len(cols)),
        out_specs=[whole] * len(shapes),
        out_shape=shapes,
        scratch_shapes=[
            pltpu.VMEM((rows, count), jnp.bfloat16),
            pltpu.VMEM((count, width), jnp.bfloat16),
            pltpu.VMEM((rows, width), jnp.float32),
        ],
        compiler_params=pltpu.CompilerParams(vmem_limit_bytes=GRANT),
        name="gram",
    )(place, *pieces, *cols)


def on_device(pulses, wind_x, wind_y, obs_tile, obs_weight, obs_precision):
    tracers = pulses.shape[0]
    cells = lax.axis_size(CELLS)
    obs = obs_tile.shape[0]
    half = tracers // 2
    pulses = pulses.reshape(tracers * 4, 128)

    messages = edges(pulses, wind_x, wind_y)
    halos = []
    for k in range(2):
        halos.append((shifted(messages[2 * k + 1], CELLS, 1), shifted(messages[2 * k], CELLS, -1)))
    sampled = None
    pulses = pltpu.with_memory_space_constraint(pulses, pltpu.HBM)
    for span, (above, below) in zip(spans(tracers), halos):
        sampled = transport(pulses, above, below, wind_x, wind_y, span, sampled)

    tile = obs_tile[:, 0]
    order = jnp.arange(obs)
    earlier = (tile[:, None] == tile[None, :]) & (order[None, :] < order[:, None])
    slot = 2 * CAP * tile + jnp.sum(earlier.astype(jnp.int32), axis=1)
    lanes = jnp.arange(2 * CAP * cells)[None, :]
    chosen = [(slot[:, None] + CAP * h == lanes).astype(jnp.bfloat16) for h in range(2)]
    wide = obs_weight.astype(jnp.float32)
    averaging = (wide / jnp.sum(wide, axis=1, keepdims=True)).astype(jnp.bfloat16)
    split = obs_weight.shape[1] // 2
    rows_out = lax.dot_general(
        jnp.concatenate(chosen, axis=0),
        jnp.concatenate([averaging[:, :split], averaging[:, split:]], axis=0),
        (((0,), (0,)), ((), ())),
        preferred_element_type=jnp.float32,
    ).astype(jnp.bfloat16)
    rows_in = exchanged(rows_out.reshape(cells, 2 * CAP, split), CELLS)

    jac_tile = jacobian(rows_in.reshape(cells * 2 * CAP, split), sampled)
    jac_back = exchanged(jac_tile.reshape(cells, 2 * CAP, half), CELLS)
    jac_back = jac_back.reshape(cells * 2 * CAP, half)
    jac = [
        lax.dot_general(
            c, jac_back, (((1,), (0,)), ((), ())), preferred_element_type=jnp.float32
        )
        for c in chosen
    ]
    precision = obs_precision.astype(jnp.float32)[:, None]
    weighted = [(precision * j).astype(jnp.bfloat16) for j in jac]
    low, high = [j.astype(jnp.bfloat16) for j in jac]

    group = lax.axis_size(XY)
    peers = lax.axis_size(TRACERS)
    here = lax.axis_index(XY)
    odd = here % 2
    pairs = [(i // peers, i % peers) for i in range(group * peers)]
    mine = jnp.where(odd == 0, low, high), jnp.where(odd == 0, high, low)
    pieces = []
    for flip in (0, 2):
        for s, value in enumerate(mine):
            path = [
                (a * peers + q, (2 * q + (a % 2 ^ s)) * peers + (a // 2 ^ flip)) for a, q in pairs
            ]
            pieces.append(lax.ppermute(value, PLANE, path))
    for k in range(4):
        pieces.append(shifted(pieces[k], "core", 1))

    deep = lax.axis_size("y")
    first_cols = exchanged(jnp.broadcast_to(weighted[0], (group, obs, half)), XY)
    value = weighted[1]
    cols = [value, shifted(value, "xl", 1)]
    for d in range(1, deep):
        cols.append(shifted(value, "y", d))
    for d in range(1, deep):
        path = [(k, (1 - k // deep) * deep + (k + d) % deep) for k in range(group)]
        cols.append(lax.ppermute(value, XY, path))
    xl, y = lax.axis_index("xl"), lax.axis_index("y")
    owners = [here, (1 - xl) * deep + y]
    owners += [xl * deep + (y - d) % deep for d in range(1, deep)]
    owners += [(1 - xl) * deep + (y - d) % deep for d in range(1, deep)]
    tracer = lax.axis_index(TRACERS)
    row_owners = [2 * (tracer ^ flip) + (odd ^ s) for flip in (0, 2, 1, 3) for s in (0, 1)]
    place = jnp.stack(row_owners + owners + [lax.axis_index("z")]).astype(jnp.int32)

    depth = lax.axis_size("z")
    tile = gram_tile(place, pieces, [first_cols.reshape(group * obs, half)], 0)[0]
    parts = exchanged(tile.reshape(depth, half // depth, half), "z")
    total = jnp.sum(parts.astype(jnp.float32), axis=0)
    blocks = gram_tile(place, pieces, cols, depth)
    last = blocks[0]
    for d in (4, 3, 5, 2, 6, 1, 7):
        last = last + shifted(blocks[d], "z", d).astype(jnp.float32)
    return jnp.concatenate([total, last], axis=1)


def solution(mesh):
    fine = Mesh(mesh.devices.reshape(2, 4, 8, 2, 2), CELLS + TRACERS)
    placed = (
        P(TRACERS, CELLS, None),
        P(CELLS, None),
        P(CELLS, None),
        P(CELLS, None),
        P(CELLS, None),
        P(CELLS),
    )
    return jax.shard_map(
        on_device, mesh=fine, in_specs=placed, out_specs=P(CELLS, TRACERS), check_vma=False
    )
```

```python
import functools

import jax
import jax.numpy as jnp
from jax import lax
from jax.experimental import pallas as pl
from jax.experimental.pallas import tpu as pltpu
from jax.sharding import Mesh, PartitionSpec as P


STEPS = 3
GRANT = 16 * 1024 * 1024
CAP = 4
XY = ("xl", "y")
CELLS = ("xl", "y", "z")
TRACERS = ("xh", "core")
PLANE = XY + TRACERS


def shifted(value, axis, steps):
    count = lax.axis_size(axis)
    return lax.ppermute(value, axis, [(i, (i + steps) % count) for i in range(count)])


def exchanged(value, axis):
    return lax.all_to_all(value, axis, split_axis=0, concat_axis=0, tiled=True)


def edge_rows(pulse_ref, wind_x_ref, wind_y_ref, *out_refs):
    tracers = pulse_ref.shape[0] // 4
    rows = [pulse_ref[pl.ds(r, tracers, 4), :].astype(jnp.bfloat16) for r in range(4)]
    winds = jnp.concatenate([wind_x_ref[...], wind_y_ref[...]], axis=0)
    coarse = winds.astype(jnp.bfloat16).astype(jnp.float32)
    both = jnp.concatenate([coarse, winds - coarse], axis=0).astype(jnp.bfloat16)
    for k, (start, size) in enumerate(spans(tracers)):
        for edge in range(2):
            ref = out_refs[2 * k + edge]
            for r in range(STEPS):
                ref[r * size : (r + 1) * size] = rows[r + edge][start : start + size]
            ref[STEPS * size :] = both


def spans(tracers):
    cut = tracers * 3 // 4
    return [(0, cut), (cut, tracers - cut)]


def edges(pulses, wind_x, wind_y):
    tracers = pulses.shape[0] // 4
    shapes = []
    for start, size in spans(tracers):
        shapes += [jax.ShapeDtypeStruct((STEPS * size + 16, 128), jnp.bfloat16)] * 2
    return pl.pallas_call(edge_rows, out_shape=shapes, name="edges")(pulses, wind_x, wind_y)


PIECE = 64


def transport_body(
    pulse_ref, a0, a1, a2, b0, b1, b2, a_winds, b_winds, wind_x_ref, wind_y_ref, *refs
):
    out_ref, coef_ref = refs[-2:]
    count = out_ref.shape[0]

    @pl.when(pl.program_id(0) == 0)
    def _():
        above = a_winds[...].astype(jnp.float32)
        below = b_winds[...].astype(jnp.float32)
        above = above[0:8] + above[8:16]
        below = below[0:8] + below[8:16]
        wind_x = jnp.concatenate([above[2:4], wind_x_ref[...], below[0:2]], axis=0)
        wind_y = jnp.concatenate([above[6:8], wind_y_ref[...], below[4:6]], axis=0)
        next_y = jnp.concatenate([above[7:8], wind_y_ref[...], below[4:7]], axis=0)
        gain_x, loss_x = jnp.maximum(wind_x, 0.0), jnp.minimum(wind_x, 0.0)
        gain_y, loss_y = jnp.maximum(wind_y, 0.0), jnp.minimum(wind_y, 0.0)
        keep = 1.0 + loss_x - pltpu.roll(gain_x, 127, 1) + loss_y - jnp.maximum(next_y, 0.0)
        parts = [
            keep, gain_x, -pltpu.roll(loss_x, 127, 1), gain_y, -jnp.minimum(next_y, 0.0)
        ]
        for k, part in enumerate(parts):
            for w in range(8):
                coef_ref[k * 8 + w] = jnp.broadcast_to(part[w : w + 1], (PIECE, 128))

    for piece in range(count // PIECE):
        at = piece * PIECE
        field = (
            [ref[at : at + PIECE].astype(jnp.float32) for ref in (a0, a1, a2)]
            + [pulse_ref[pl.ds(4 * at + r, PIECE, 4), :] for r in range(4)]
            + [ref[at : at + PIECE].astype(jnp.float32) for ref in (b0, b1, b2)]
        )
        for step in range(STEPS):
            new = []
            for i in range(len(field) - 2):
                w = step + i
                here = field[i + 1]
                new.append(
                    coef_ref[w] * here
                    + coef_ref[8 + w] * pltpu.roll(here, 1, 1)
                    + coef_ref[16 + w] * pltpu.roll(here, 127, 1)
                    + coef_ref[24 + w] * field[i]
                    + coef_ref[32 + w] * field[i + 2]
                )
            field = new
        for r in range(4):
            out_ref[at : at + PIECE, r * 128 : (r + 1) * 128] = field[r].astype(jnp.bfloat16)


def transport(pulses, above, below, wind_x, wind_y, span, into=None, block=256):
    tracers = pulses.shape[0] // 4
    start, size = span
    skip, steps = start // block, size // block
    halo = [
        pl.BlockSpec((block, 128), lambda i, r=r: (r * steps + i, 0)) for r in range(STEPS)
    ]
    last = [pl.BlockSpec((16, 128), lambda i: (STEPS * size // 16, 0))] * 2
    wind = pl.BlockSpec((4, 128), lambda i: (0, 0))
    operands = [pulses, *[above] * 3, *[below] * 3, above, below, wind_x, wind_y]
    specs = [pl.BlockSpec((4 * block, 128), lambda i: (skip + i, 0))] + halo + halo + last
    specs += [wind, wind]
    aliases = {}
    if into is not None:
        aliases = {len(operands): 0}
        operands.append(into)
        specs.append(pl.BlockSpec(memory_space=pl.ANY))
    return pl.pallas_call(
        transport_body,
        grid=(steps,),
        in_specs=specs,
        out_specs=pl.BlockSpec((block, 512), lambda i: (skip + i, 0)),
        out_shape=jax.ShapeDtypeStruct((tracers, 512), jnp.bfloat16),
        scratch_shapes=[
            pltpu.VMEM((40, PIECE, 128), jnp.float32),
        ],
        input_output_aliases=aliases,
        compiler_params=pltpu.CompilerParams(vmem_limit_bytes=GRANT),
        name="transport",
    )(*operands)


def jacobian_body(rows_ref, low_ref, high_ref, out_ref, full_ref):
    @pl.when(pl.program_id(0) == 0)
    def _():
        count, width = rows_ref.shape
        mine = rows_ref[...].astype(jnp.float32).reshape(count // 8, 8, width)
        swap = pltpu.roll(mine, 4, 1)
        top = lax.broadcasted_iota(jnp.int32, mine.shape, 1) < 4
        left = jnp.where(top, mine, swap).reshape(count, width)
        right = jnp.where(top, swap, mine).reshape(count, width)
        full_ref[:, :width] = left.astype(jnp.bfloat16)
        full_ref[:, width:] = right.astype(jnp.bfloat16)

    dims = (((1,), (1,)), ((), ()))
    full = full_ref[...]
    low = lax.dot_general(full, low_ref[...], dims, preferred_element_type=jnp.float32)
    high = lax.dot_general(full, high_ref[...], dims, preferred_element_type=jnp.float32)
    row = lax.broadcasted_iota(jnp.int32, low.shape, 0)
    out_ref[...] = jnp.where((row & 4) == 0, low, high).astype(jnp.bfloat16)


def jacobian(rows, sampled, block=256):
    tracers = sampled.shape[0]
    count, width = rows.shape
    steps = tracers // 2 // block
    return pl.pallas_call(
        jacobian_body,
        grid=(steps,),
        in_specs=[
            pl.BlockSpec((count, width), lambda i: (0, 0)),
            pl.BlockSpec((block, 512), lambda i: (i, 0)),
            pl.BlockSpec((block, 512), lambda i: (steps + i, 0)),
        ],
        out_specs=pl.BlockSpec((count, block), lambda i: (0, i)),
        out_shape=jax.ShapeDtypeStruct((count, tracers // 2), jnp.bfloat16),
        scratch_shapes=[pltpu.VMEM((count, 2 * width), jnp.bfloat16)],
        compiler_params=pltpu.CompilerParams(vmem_limit_bytes=GRANT),
        name="jacobian",
    )(rows, sampled, sampled)


def gram_body(apart, place_ref, same_ref, cross_ref, across_ref, other_ref, *refs):
    cols, outs, scratch = refs[:8], refs[8:-3], refs[-3:]
    rows_ref, cols_ref, sum_ref = scratch
    block = same_ref.shape[0]
    parts = [same_ref[...], cross_ref[...]]
    for ref in (across_ref, other_ref):
        parts += [ref[s : s + block] for s in range(0, ref.shape[0], block)]
    for k, part in enumerate(parts):
        at = pl.multiple_of(place_ref[k] * block, block)
        rows_ref[:, pl.ds(at, block)] = part.T
    for k, ref in enumerate(cols):
        at = pl.multiple_of(place_ref[8 + k] * block, block)
        cols_ref[pl.ds(at, block), :] = ref[...]
    tile = lax.dot_general(
        rows_ref[...], cols_ref[...], (((1,), (0,)), ((), ())), preferred_element_type=jnp.float32
    )
    if not apart:
        outs[0][...] = tile.astype(jnp.bfloat16)
        return
    sum_ref[...] = tile
    deep = len(outs)
    size = tile.shape[0] // deep
    for d, out_ref in enumerate(outs):
        at = pl.multiple_of(((place_ref[16] + d) % deep) * size, size)
        out_ref[...] = sum_ref[pl.ds(at, size), :].astype(out_ref.dtype)


def gram_tile(place, same, cross, across, other, cols, apart):
    obs, width = cols[0].shape
    rows = same.shape[1]
    if apart:
        size = (rows // apart, width)
        shapes = [jax.ShapeDtypeStruct(size, jnp.float32)]
        shapes += [jax.ShapeDtypeStruct(size, jnp.bfloat16)] * (apart - 1)
    else:
        shapes = [jax.ShapeDtypeStruct((rows, width), jnp.bfloat16)]
    whole = pl.BlockSpec(memory_space=pltpu.VMEM)
    return pl.pallas_call(
        functools.partial(gram_body, apart),
        in_specs=[pl.BlockSpec(memory_space=pltpu.SMEM)] + [whole] * (4 + len(cols)),
        out_specs=[whole] * len(shapes),
        out_shape=shapes,
        scratch_shapes=[
            pltpu.VMEM((rows, len(cols) * obs), jnp.bfloat16),
            pltpu.VMEM((len(cols) * obs, width), jnp.bfloat16),
            pltpu.VMEM((rows, width), jnp.float32),
        ],
        compiler_params=pltpu.CompilerParams(vmem_limit_bytes=GRANT),
        name="gram",
    )(place, same, cross, across, other, *cols)


def on_device(pulses, wind_x, wind_y, obs_tile, obs_weight, obs_precision):
    tracers = pulses.shape[0]
    cells = lax.axis_size(CELLS)
    obs = obs_tile.shape[0]
    half = tracers // 2
    pulses = pulses.reshape(tracers * 4, 128)

    messages = edges(pulses, wind_x, wind_y)
    halos = []
    for k in range(2):
        halos.append((shifted(messages[2 * k + 1], CELLS, 1), shifted(messages[2 * k], CELLS, -1)))
    sampled = None
    pulses = pltpu.with_memory_space_constraint(pulses, pltpu.HBM)
    for span, (above, below) in zip(spans(tracers), halos):
        sampled = transport(pulses, above, below, wind_x, wind_y, span, sampled)

    tile = obs_tile[:, 0]
    order = jnp.arange(obs)
    earlier = (tile[:, None] == tile[None, :]) & (order[None, :] < order[:, None])
    slot = 2 * CAP * tile + jnp.sum(earlier.astype(jnp.int32), axis=1)
    lanes = jnp.arange(2 * CAP * cells)[None, :]
    chosen = [(slot[:, None] + CAP * h == lanes).astype(jnp.bfloat16) for h in range(2)]
    wide = obs_weight.astype(jnp.float32)
    averaging = (wide / jnp.sum(wide, axis=1, keepdims=True)).astype(jnp.bfloat16)
    split = obs_weight.shape[1] // 2
    rows_out = lax.dot_general(
        jnp.concatenate(chosen, axis=0),
        jnp.concatenate([averaging[:, :split], averaging[:, split:]], axis=0),
        (((0,), (0,)), ((), ())),
        preferred_element_type=jnp.float32,
    ).astype(jnp.bfloat16)
    rows_in = exchanged(rows_out.reshape(cells, 2 * CAP, split), CELLS)

    jac_tile = jacobian(rows_in.reshape(cells * 2 * CAP, split), sampled)
    precision = obs_precision.astype(jnp.float32)[:, None]
    jac_tile, precision = lax.optimization_barrier((jac_tile, precision))
    jac_back = exchanged(jac_tile.reshape(cells, 2 * CAP, half), CELLS)
    jac_back = jac_back.reshape(cells * 2 * CAP, half)
    jac = [
        lax.dot_general(
            c, jac_back, (((1,), (0,)), ((), ())), preferred_element_type=jnp.float32
        )
        for c in chosen
    ]
    weighted = [(precision * j).astype(jnp.bfloat16) for j in jac]
    low, high = [j.astype(jnp.bfloat16) for j in jac]

    group = lax.axis_size(XY)
    peers = lax.axis_size(TRACERS)
    here = lax.axis_index(XY)
    odd = here % 2
    pairs = [(i // peers, i % peers) for i in range(group * peers)]
    to_same = [(a * peers + q, (2 * q + a % 2) * peers + a // 2) for a, q in pairs]
    to_cross = [(a * peers + q, (2 * q + 1 - a % 2) * peers + a // 2) for a, q in pairs]
    same = lax.ppermute(jnp.where(odd == 0, low, high), PLANE, to_same)
    cross = lax.ppermute(jnp.where(odd == 0, high, low), PLANE, to_cross)
    across = shifted(jnp.concatenate([same, cross], axis=0), "xh", 1)
    other = shifted(jnp.concatenate([same, cross, across], axis=0), "core", 1)

    deep = lax.axis_size("y")
    cols = []
    for part, value in enumerate(weighted):
        beside = shifted(value, "xl", 1)
        cols.append([value, beside])
        for source in (value, beside):
            for d in range(1, deep):
                cols[part].append(shifted(source, "y", d))
    xl, y = lax.axis_index("xl"), lax.axis_index("y")
    owners = [here, (1 - xl) * deep + y]
    owners += [xl * deep + (y - d) % deep for d in range(1, deep)]
    owners += [(1 - xl) * deep + (y - d) % deep for d in range(1, deep)]
    tracer = lax.axis_index(TRACERS)
    row_owners = [2 * (tracer ^ flip) + (odd ^ s) for flip in (0, 2, 1, 3) for s in (0, 1)]
    place = jnp.stack(row_owners + owners + [lax.axis_index("z")]).astype(jnp.int32)

    depth = lax.axis_size("z")
    tile = gram_tile(place, same, cross, across, other, cols[0], 0)[0]
    parts = exchanged(tile.reshape(depth, half // depth, half), "z")
    total = jnp.sum(parts.astype(jnp.float32), axis=0)
    blocks = gram_tile(place, same, cross, across, other, cols[1], depth)
    last = blocks[0]
    for d in (4, 3, 5, 2, 6, 1, 7):
        last = last + shifted(blocks[d], "z", d).astype(jnp.float32)
    return jnp.concatenate([total, last], axis=1)


def solution(mesh):
    fine = Mesh(mesh.devices.reshape(2, 4, 8, 2, 2), CELLS + TRACERS)
    placed = (
        P(TRACERS, CELLS, None),
        P(CELLS, None),
        P(CELLS, None),
        P(CELLS, None),
        P(CELLS, None),
        P(CELLS),
    )
    return jax.shard_map(
        on_device, mesh=fine, in_specs=placed, out_specs=P(CELLS, TRACERS), check_vma=False
    )
```

```python
import functools

import jax
import jax.numpy as jnp
from jax import lax
from jax.experimental import pallas as pl
from jax.experimental.pallas import tpu as pltpu
from jax.sharding import Mesh, PartitionSpec as P


STEPS = 3
GRANT = 16 * 1024 * 1024
CAP = 4
XY = ("xl", "y")
CELLS = ("xl", "y", "z")
TRACERS = ("xh", "core")
PLANE = XY + TRACERS


def shifted(value, axis, steps):
    count = lax.axis_size(axis)
    return lax.ppermute(value, axis, [(i, (i + steps) % count) for i in range(count)])


def exchanged(value, axis):
    return lax.all_to_all(value, axis, split_axis=0, concat_axis=0, tiled=True)


def edge_rows(pulse_ref, wind_x_ref, wind_y_ref, *out_refs):
    tracers = pulse_ref.shape[0] // 4
    rows = [pulse_ref[pl.ds(r, tracers, 4), :].astype(jnp.bfloat16) for r in range(4)]
    winds = jnp.concatenate([wind_x_ref[...], wind_y_ref[...]], axis=0)
    coarse = winds.astype(jnp.bfloat16).astype(jnp.float32)
    both = jnp.concatenate([coarse, winds - coarse], axis=0).astype(jnp.bfloat16)
    for k, (start, size) in enumerate(spans(tracers)):
        for edge in range(2):
            ref = out_refs[2 * k + edge]
            for r in range(STEPS):
                ref[r * size : (r + 1) * size] = rows[r + edge][start : start + size]
            ref[STEPS * size :] = both


def spans(tracers):
    cut = tracers * 3 // 4
    return [(0, cut), (cut, tracers - cut)]


def edges(pulses, wind_x, wind_y):
    tracers = pulses.shape[0] // 4
    shapes = []
    for start, size in spans(tracers):
        shapes += [jax.ShapeDtypeStruct((STEPS * size + 16, 128), jnp.bfloat16)] * 2
    return pl.pallas_call(edge_rows, out_shape=shapes, name="edges")(pulses, wind_x, wind_y)


PIECE = 64


def transport_body(
    pulse_ref, a0, a1, a2, b0, b1, b2, a_winds, b_winds, wind_x_ref, wind_y_ref, *refs
):
    out_ref, coef_ref = refs[-2:]
    count = out_ref.shape[0]

    @pl.when(pl.program_id(0) == 0)
    def _():
        above = a_winds[...].astype(jnp.float32)
        below = b_winds[...].astype(jnp.float32)
        above = above[0:8] + above[8:16]
        below = below[0:8] + below[8:16]
        wind_x = jnp.concatenate([above[2:4], wind_x_ref[...], below[0:2]], axis=0)
        wind_y = jnp.concatenate([above[6:8], wind_y_ref[...], below[4:6]], axis=0)
        next_y = jnp.concatenate([above[7:8], wind_y_ref[...], below[4:7]], axis=0)
        gain_x, loss_x = jnp.maximum(wind_x, 0.0), jnp.minimum(wind_x, 0.0)
        gain_y, loss_y = jnp.maximum(wind_y, 0.0), jnp.minimum(wind_y, 0.0)
        keep = 1.0 + loss_x - pltpu.roll(gain_x, 127, 1) + loss_y - jnp.maximum(next_y, 0.0)
        parts = [
            keep, gain_x, -pltpu.roll(loss_x, 127, 1), gain_y, -jnp.minimum(next_y, 0.0)
        ]
        for k, part in enumerate(parts):
            for w in range(8):
                coef_ref[k * 8 + w] = jnp.broadcast_to(part[w : w + 1], (PIECE, 128))

    for piece in range(count // PIECE):
        at = piece * PIECE
        field = (
            [ref[at : at + PIECE].astype(jnp.float32) for ref in (a0, a1, a2)]
            + [pulse_ref[pl.ds(4 * at + r, PIECE, 4), :] for r in range(4)]
            + [ref[at : at + PIECE].astype(jnp.float32) for ref in (b0, b1, b2)]
        )
        for step in range(STEPS):
            new = []
            for i in range(len(field) - 2):
                w = step + i
                here = field[i + 1]
                new.append(
                    coef_ref[w] * here
                    + coef_ref[8 + w] * pltpu.roll(here, 1, 1)
                    + coef_ref[16 + w] * pltpu.roll(here, 127, 1)
                    + coef_ref[24 + w] * field[i]
                    + coef_ref[32 + w] * field[i + 2]
                )
            field = new
        for r in range(4):
            out_ref[at : at + PIECE, r * 128 : (r + 1) * 128] = field[r].astype(jnp.bfloat16)


def transport(pulses, above, below, wind_x, wind_y, span, into=None, block=256):
    tracers = pulses.shape[0] // 4
    start, size = span
    skip, steps = start // block, size // block
    halo = [
        pl.BlockSpec((block, 128), lambda i, r=r: (r * steps + i, 0)) for r in range(STEPS)
    ]
    last = [pl.BlockSpec((16, 128), lambda i: (STEPS * size // 16, 0))] * 2
    wind = pl.BlockSpec((4, 128), lambda i: (0, 0))
    operands = [pulses, *[above] * 3, *[below] * 3, above, below, wind_x, wind_y]
    specs = [pl.BlockSpec((4 * block, 128), lambda i: (skip + i, 0))] + halo + halo + last
    specs += [wind, wind]
    aliases = {}
    if into is not None:
        aliases = {len(operands): 0}
        operands.append(into)
        specs.append(pl.BlockSpec(memory_space=pl.ANY))
    return pl.pallas_call(
        transport_body,
        grid=(steps,),
        in_specs=specs,
        out_specs=pl.BlockSpec((block, 512), lambda i: (skip + i, 0)),
        out_shape=jax.ShapeDtypeStruct((tracers, 512), jnp.bfloat16),
        scratch_shapes=[
            pltpu.VMEM((40, PIECE, 128), jnp.float32),
        ],
        input_output_aliases=aliases,
        compiler_params=pltpu.CompilerParams(vmem_limit_bytes=GRANT),
        name="transport",
    )(*operands)


def jacobian_body(rows_ref, low_ref, high_ref, out_ref, full_ref):
    @pl.when(pl.program_id(0) == 0)
    def _():
        count, width = rows_ref.shape
        mine = rows_ref[...].astype(jnp.float32).reshape(count // 8, 8, width)
        swap = pltpu.roll(mine, 4, 1)
        top = lax.broadcasted_iota(jnp.int32, mine.shape, 1) < 4
        left = jnp.where(top, mine, swap).reshape(count, width)
        right = jnp.where(top, swap, mine).reshape(count, width)
        full_ref[:, :width] = left.astype(jnp.bfloat16)
        full_ref[:, width:] = right.astype(jnp.bfloat16)

    dims = (((1,), (1,)), ((), ()))
    full = full_ref[...]
    low = lax.dot_general(full, low_ref[...], dims, preferred_element_type=jnp.float32)
    high = lax.dot_general(full, high_ref[...], dims, preferred_element_type=jnp.float32)
    row = lax.broadcasted_iota(jnp.int32, low.shape, 0)
    out_ref[...] = jnp.where((row & 4) == 0, low, high).astype(jnp.bfloat16)


def jacobian(rows, sampled, block=256):
    tracers = sampled.shape[0]
    count, width = rows.shape
    steps = tracers // 2 // block
    return pl.pallas_call(
        jacobian_body,
        grid=(steps,),
        in_specs=[
            pl.BlockSpec((count, width), lambda i: (0, 0)),
            pl.BlockSpec((block, 512), lambda i: (i, 0)),
            pl.BlockSpec((block, 512), lambda i: (steps + i, 0)),
        ],
        out_specs=pl.BlockSpec((count, block), lambda i: (0, i)),
        out_shape=jax.ShapeDtypeStruct((count, tracers // 2), jnp.bfloat16),
        scratch_shapes=[pltpu.VMEM((count, 2 * width), jnp.bfloat16)],
        compiler_params=pltpu.CompilerParams(vmem_limit_bytes=GRANT),
        name="jacobian",
    )(rows, sampled, sampled)


def gram_body(apart, place_ref, same_ref, cross_ref, across_ref, other_ref, *refs):
    cols, outs, scratch = refs[:8], refs[8:-3], refs[-3:]
    rows_ref, cols_ref, sum_ref = scratch
    block = same_ref.shape[0]
    parts = [same_ref[...], cross_ref[...]]
    for ref in (across_ref, other_ref):
        parts += [ref[s : s + block] for s in range(0, ref.shape[0], block)]
    for k, part in enumerate(parts):
        at = pl.multiple_of(place_ref[k] * block, block)
        rows_ref[:, pl.ds(at, block)] = part.T
    for k, ref in enumerate(cols):
        at = pl.multiple_of(place_ref[8 + k] * block, block)
        cols_ref[pl.ds(at, block), :] = ref[...]
    tile = lax.dot_general(
        rows_ref[...], cols_ref[...], (((1,), (0,)), ((), ())), preferred_element_type=jnp.float32
    )
    if not apart:
        outs[0][...] = tile.astype(jnp.bfloat16)
        return
    sum_ref[...] = tile
    deep = len(outs)
    size = tile.shape[0] // deep
    for d, out_ref in enumerate(outs):
        at = pl.multiple_of(((place_ref[16] + d) % deep) * size, size)
        out_ref[...] = sum_ref[pl.ds(at, size), :].astype(out_ref.dtype)


def gram_tile(place, same, cross, across, other, cols, apart):
    obs, width = cols[0].shape
    rows = same.shape[1]
    if apart:
        size = (rows // apart, width)
        shapes = [jax.ShapeDtypeStruct(size, jnp.float32)]
        shapes += [jax.ShapeDtypeStruct(size, jnp.bfloat16)] * (apart - 1)
    else:
        shapes = [jax.ShapeDtypeStruct((rows, width), jnp.bfloat16)]
    whole = pl.BlockSpec(memory_space=pltpu.VMEM)
    return pl.pallas_call(
        functools.partial(gram_body, apart),
        in_specs=[pl.BlockSpec(memory_space=pltpu.SMEM)] + [whole] * (4 + len(cols)),
        out_specs=[whole] * len(shapes),
        out_shape=shapes,
        scratch_shapes=[
            pltpu.VMEM((rows, len(cols) * obs), jnp.bfloat16),
            pltpu.VMEM((len(cols) * obs, width), jnp.bfloat16),
            pltpu.VMEM((rows, width), jnp.float32),
        ],
        compiler_params=pltpu.CompilerParams(vmem_limit_bytes=GRANT),
        name="gram",
    )(place, same, cross, across, other, *cols)


def on_device(pulses, wind_x, wind_y, obs_tile, obs_weight, obs_precision):
    tracers = pulses.shape[0]
    cells = lax.axis_size(CELLS)
    obs = obs_tile.shape[0]
    half = tracers // 2
    pulses = pulses.reshape(tracers * 4, 128)

    messages = edges(pulses, wind_x, wind_y)
    halos = []
    for k in range(2):
        halos.append((shifted(messages[2 * k + 1], CELLS, 1), shifted(messages[2 * k], CELLS, -1)))
    sampled = None
    pulses = pltpu.with_memory_space_constraint(pulses, pltpu.HBM)
    for span, (above, below) in zip(spans(tracers), halos):
        sampled = transport(pulses, above, below, wind_x, wind_y, span, sampled)

    tile = obs_tile[:, 0]
    order = jnp.arange(obs)
    earlier = (tile[:, None] == tile[None, :]) & (order[None, :] < order[:, None])
    slot = 2 * CAP * tile + jnp.sum(earlier.astype(jnp.int32), axis=1)
    lanes = jnp.arange(2 * CAP * cells)[None, :]
    chosen = [(slot[:, None] + CAP * h == lanes).astype(jnp.bfloat16) for h in range(2)]
    wide = obs_weight.astype(jnp.float32)
    averaging = (wide / jnp.sum(wide, axis=1, keepdims=True)).astype(jnp.bfloat16)
    split = obs_weight.shape[1] // 2
    rows_out = lax.dot_general(
        jnp.concatenate(chosen, axis=0),
        jnp.concatenate([averaging[:, :split], averaging[:, split:]], axis=0),
        (((0,), (0,)), ((), ())),
        preferred_element_type=jnp.float32,
    ).astype(jnp.bfloat16)
    rows_in = exchanged(rows_out.reshape(cells, 2 * CAP, split), CELLS)

    jac_tile = jacobian(rows_in.reshape(cells * 2 * CAP, split), sampled)
    group = lax.axis_size(XY)
    peers = lax.axis_size(TRACERS)
    deep = lax.axis_size("y")
    here = lax.axis_index(XY)
    odd = here % 2
    xl, y = lax.axis_index("xl"), lax.axis_index("y")
    owners = [here, (1 - xl) * deep + y]
    owners += [xl * deep + (y - d) % deep for d in range(1, deep)]
    owners += [(1 - xl) * deep + (y - d) % deep for d in range(1, deep)]
    tracer = lax.axis_index(TRACERS)
    row_owners = [2 * (tracer ^ flip) + (odd ^ s) for flip in (0, 2, 1, 3) for s in (0, 1)]
    place = jnp.stack(row_owners + owners + [lax.axis_index("z")]).astype(jnp.int32)
    precision = obs_precision.astype(jnp.float32)[:, None]
    even = odd == 0
    jac_tile, precision, place, even = lax.optimization_barrier((jac_tile, precision, place, even))
    jac_back = exchanged(jac_tile.reshape(cells, 2 * CAP, half), CELLS)
    jac_back = jac_back.reshape(cells * 2 * CAP, half)
    jac = [
        lax.dot_general(
            c, jac_back, (((1,), (0,)), ((), ())), preferred_element_type=jnp.float32
        )
        for c in chosen
    ]
    weighted = [(precision * j).astype(jnp.bfloat16) for j in jac]
    low, high = [j.astype(jnp.bfloat16) for j in jac]

    pairs = [(i // peers, i % peers) for i in range(group * peers)]
    to_same = [(a * peers + q, (2 * q + a % 2) * peers + a // 2) for a, q in pairs]
    to_cross = [(a * peers + q, (2 * q + 1 - a % 2) * peers + a // 2) for a, q in pairs]
    same = lax.ppermute(jnp.where(even, low, high), PLANE, to_same)
    cross = lax.ppermute(jnp.where(even, high, low), PLANE, to_cross)
    across = shifted(jnp.concatenate([same, cross], axis=0), "xh", 1)
    other = shifted(jnp.concatenate([same, cross, across], axis=0), "core", 1)

    cols = []
    for part, value in enumerate(weighted):
        beside = shifted(value, "xl", 1)
        cols.append([value, beside])
        for source in (value, beside):
            for d in range(1, deep):
                cols[part].append(shifted(source, "y", d))

    depth = lax.axis_size("z")
    tile = gram_tile(place, same, cross, across, other, cols[0], 0)[0]
    parts = exchanged(tile.reshape(depth, half // depth, half), "z")
    total = jnp.sum(parts.astype(jnp.float32), axis=0)
    blocks = gram_tile(place, same, cross, across, other, cols[1], depth)
    last = blocks[0]
    for d in (4, 3, 5, 2, 6, 1, 7):
        last = last + shifted(blocks[d], "z", d).astype(jnp.float32)
    return jnp.concatenate([total, last], axis=1)


def solution(mesh):
    fine = Mesh(mesh.devices.reshape(2, 4, 8, 2, 2), CELLS + TRACERS)
    placed = (
        P(TRACERS, CELLS, None),
        P(CELLS, None),
        P(CELLS, None),
        P(CELLS, None),
        P(CELLS, None),
        P(CELLS),
    )
    return jax.shard_map(
        on_device, mesh=fine, in_specs=placed, out_specs=P(CELLS, TRACERS), check_vma=False
    )
```

```python
import functools

import jax
import jax.numpy as jnp
from jax import lax
from jax.experimental import pallas as pl
from jax.experimental.pallas import tpu as pltpu
from jax.sharding import Mesh, PartitionSpec as P


STEPS = 3
CHUNKS = 4
GRANT = 16 * 1024 * 1024
CAP = 4
XY = ("xl", "y")
CELLS = ("xl", "y", "z")
TRACERS = ("xh", "core")
PLANE = XY + TRACERS


def shifted(value, axis, steps):
    count = lax.axis_size(axis)
    return lax.ppermute(value, axis, [(i, (i + steps) % count) for i in range(count)])


def exchanged(value, axis):
    return lax.all_to_all(value, axis, split_axis=0, concat_axis=0, tiled=True)


def edge_rows(pulse_ref, wind_x_ref, wind_y_ref, *refs):
    out_refs, (fetched_ref, winds_ref, sems) = refs[:-3], refs[-3:]
    tracers = pulse_ref.shape[0] // 4
    size = tracers // CHUNKS
    copies = []
    for k in range(CHUNKS):
        part = pl.ds(4 * k * size, 4 * size)
        copies.append(
            pltpu.make_async_copy(pulse_ref.at[part], fetched_ref.at[part], sems.at[k])
        )
    for k, ref in enumerate((wind_x_ref, wind_y_ref)):
        copies.append(pltpu.make_async_copy(ref, winds_ref.at[k], sems.at[CHUNKS + k]))
    for copy in copies:
        copy.start()
    for k in range(CHUNKS):
        copies[k].wait()
        rows = [
            fetched_ref[pl.ds(4 * k * size + r, size, 4), :].astype(jnp.bfloat16) for r in range(4)
        ]
        for part, (start, length) in enumerate(spans(tracers)):
            at = k * size - start
            if 0 <= at < length:
                for edge in range(2):
                    for r in range(STEPS):
                        out_refs[2 * part + edge][r * length + at : r * length + at + size] = rows[
                            r + edge
                        ]
    copies[CHUNKS].wait()
    copies[CHUNKS + 1].wait()
    winds = jnp.concatenate([winds_ref[0], winds_ref[1]], axis=0)
    coarse = winds.astype(jnp.bfloat16).astype(jnp.float32)
    both = jnp.concatenate([coarse, winds - coarse], axis=0).astype(jnp.bfloat16)
    for ref in out_refs:
        ref[ref.shape[0] - 16 :] = both


def spans(tracers):
    cut = tracers * 3 // 4
    return [(0, cut), (cut, tracers - cut)]


def edges(pulses, wind_x, wind_y):
    tracers = pulses.shape[0] // 4
    shapes = []
    for start, size in spans(tracers):
        shapes += [jax.ShapeDtypeStruct((STEPS * size + 16, 128), jnp.bfloat16)] * 2
    winds = [pltpu.with_memory_space_constraint(w, pltpu.HBM) for w in (wind_x, wind_y)]
    return pl.pallas_call(
        edge_rows,
        in_specs=[pl.BlockSpec(memory_space=pltpu.HBM)] * 3,
        out_specs=[pl.BlockSpec(memory_space=pltpu.VMEM)] * len(shapes),
        out_shape=shapes,
        scratch_shapes=[
            pltpu.VMEM(pulses.shape, jnp.float32),
            pltpu.VMEM((2, *wind_x.shape), jnp.float32),
            pltpu.SemaphoreType.DMA((CHUNKS + 2,)),
        ],
        compiler_params=pltpu.CompilerParams(vmem_limit_bytes=GRANT),
        name="edges",
    )(pulses, *winds)


PIECE = 64


def transport_body(
    pulse_ref, a0, a1, a2, b0, b1, b2, a_winds, b_winds, wind_x_ref, wind_y_ref, *refs
):
    out_ref, coef_ref = refs[-2:]
    count = out_ref.shape[0]

    @pl.when(pl.program_id(0) == 0)
    def _():
        above = a_winds[...].astype(jnp.float32)
        below = b_winds[...].astype(jnp.float32)
        above = above[0:8] + above[8:16]
        below = below[0:8] + below[8:16]
        wind_x = jnp.concatenate([above[2:4], wind_x_ref[...], below[0:2]], axis=0)
        wind_y = jnp.concatenate([above[6:8], wind_y_ref[...], below[4:6]], axis=0)
        next_y = jnp.concatenate([above[7:8], wind_y_ref[...], below[4:7]], axis=0)
        gain_x, loss_x = jnp.maximum(wind_x, 0.0), jnp.minimum(wind_x, 0.0)
        gain_y, loss_y = jnp.maximum(wind_y, 0.0), jnp.minimum(wind_y, 0.0)
        keep = 1.0 + loss_x - pltpu.roll(gain_x, 127, 1) + loss_y - jnp.maximum(next_y, 0.0)
        parts = [
            keep, gain_x, -pltpu.roll(loss_x, 127, 1), gain_y, -jnp.minimum(next_y, 0.0)
        ]
        for k, part in enumerate(parts):
            for w in range(8):
                coef_ref[k * 8 + w] = jnp.broadcast_to(part[w : w + 1], (PIECE, 128))

    for piece in range(count // PIECE):
        at = piece * PIECE
        field = (
            [ref[at : at + PIECE].astype(jnp.float32) for ref in (a0, a1, a2)]
            + [pulse_ref[pl.ds(4 * at + r, PIECE, 4), :] for r in range(4)]
            + [ref[at : at + PIECE].astype(jnp.float32) for ref in (b0, b1, b2)]
        )
        for step in range(STEPS):
            new = []
            for i in range(len(field) - 2):
                w = step + i
                here = field[i + 1]
                new.append(
                    coef_ref[w] * here
                    + coef_ref[8 + w] * pltpu.roll(here, 1, 1)
                    + coef_ref[16 + w] * pltpu.roll(here, 127, 1)
                    + coef_ref[24 + w] * field[i]
                    + coef_ref[32 + w] * field[i + 2]
                )
            field = new
        for r in range(4):
            out_ref[at : at + PIECE, r * 128 : (r + 1) * 128] = field[r].astype(jnp.bfloat16)


def transport(pulses, above, below, wind_x, wind_y, span, into=None, block=256):
    tracers = pulses.shape[0] // 4
    start, size = span
    skip, steps = start // block, size // block
    halo = [
        pl.BlockSpec((block, 128), lambda i, r=r: (r * steps + i, 0)) for r in range(STEPS)
    ]
    last = [pl.BlockSpec((16, 128), lambda i: (STEPS * size // 16, 0))] * 2
    wind = pl.BlockSpec((4, 128), lambda i: (0, 0))
    operands = [pulses, *[above] * 3, *[below] * 3, above, below, wind_x, wind_y]
    specs = [pl.BlockSpec((4 * block, 128), lambda i: (skip + i, 0))] + halo + halo + last
    specs += [wind, wind]
    aliases = {}
    if into is not None:
        aliases = {len(operands): 0}
        operands.append(into)
        specs.append(pl.BlockSpec(memory_space=pl.ANY))
    return pl.pallas_call(
        transport_body,
        grid=(steps,),
        in_specs=specs,
        out_specs=pl.BlockSpec((block, 512), lambda i: (skip + i, 0)),
        out_shape=jax.ShapeDtypeStruct((tracers, 512), jnp.bfloat16),
        scratch_shapes=[
            pltpu.VMEM((40, PIECE, 128), jnp.float32),
        ],
        input_output_aliases=aliases,
        compiler_params=pltpu.CompilerParams(vmem_limit_bytes=GRANT),
        name="transport",
    )(*operands)


def jacobian_body(rows_ref, low_ref, high_ref, out_ref, full_ref):
    @pl.when(pl.program_id(0) == 0)
    def _():
        count, width = rows_ref.shape
        mine = rows_ref[...].astype(jnp.float32).reshape(count // 8, 8, width)
        swap = pltpu.roll(mine, 4, 1)
        top = lax.broadcasted_iota(jnp.int32, mine.shape, 1) < 4
        left = jnp.where(top, mine, swap).reshape(count, width)
        right = jnp.where(top, swap, mine).reshape(count, width)
        full_ref[:, :width] = left.astype(jnp.bfloat16)
        full_ref[:, width:] = right.astype(jnp.bfloat16)

    dims = (((1,), (1,)), ((), ()))
    full = full_ref[...]
    low = lax.dot_general(full, low_ref[...], dims, preferred_element_type=jnp.float32)
    high = lax.dot_general(full, high_ref[...], dims, preferred_element_type=jnp.float32)
    row = lax.broadcasted_iota(jnp.int32, low.shape, 0)
    out_ref[...] = jnp.where((row & 4) == 0, low, high).astype(jnp.bfloat16)


def jacobian(rows, sampled, block=256):
    tracers = sampled.shape[0]
    count, width = rows.shape
    steps = tracers // 2 // block
    return pl.pallas_call(
        jacobian_body,
        grid=(steps,),
        in_specs=[
            pl.BlockSpec((count, width), lambda i: (0, 0)),
            pl.BlockSpec((block, 512), lambda i: (i, 0)),
            pl.BlockSpec((block, 512), lambda i: (steps + i, 0)),
        ],
        out_specs=pl.BlockSpec((count, block), lambda i: (0, i)),
        out_shape=jax.ShapeDtypeStruct((count, tracers // 2), jnp.bfloat16),
        scratch_shapes=[pltpu.VMEM((count, 2 * width), jnp.bfloat16)],
        compiler_params=pltpu.CompilerParams(vmem_limit_bytes=GRANT),
        name="jacobian",
    )(rows, sampled, sampled)


def gram_body(apart, place_ref, *refs):
    pieces, cols, outs, scratch = refs[:4], refs[4:12], refs[12:-3], refs[-3:]
    rows_ref, cols_ref, sum_ref = scratch
    block = cols[0].shape[0]
    parts = []
    for ref in pieces:
        parts += [ref[s : s + block] for s in range(0, ref.shape[0], block)]
    for k, part in enumerate(parts):
        at = pl.multiple_of(place_ref[k] * block, block)
        rows_ref[:, pl.ds(at, block)] = part.T
    for k, ref in enumerate(cols):
        at = pl.multiple_of(place_ref[8 + k] * block, block)
        cols_ref[pl.ds(at, block), :] = ref[...]
    tile = lax.dot_general(
        rows_ref[...], cols_ref[...], (((1,), (0,)), ((), ())), preferred_element_type=jnp.float32
    )
    if not apart:
        outs[0][...] = tile.astype(jnp.bfloat16)
        return
    sum_ref[...] = tile
    deep = len(outs)
    size = tile.shape[0] // deep
    for d, out_ref in enumerate(outs):
        at = pl.multiple_of(((place_ref[16] + d) % deep) * size, size)
        out_ref[...] = sum_ref[pl.ds(at, size), :].astype(out_ref.dtype)


def gram_tile(place, pieces, cols, apart):
    obs, width = cols[0].shape
    rows = pieces[0].shape[1]
    if apart:
        size = (rows // apart, width)
        shapes = [jax.ShapeDtypeStruct(size, jnp.float32)]
        shapes += [jax.ShapeDtypeStruct(size, jnp.bfloat16)] * (apart - 1)
    else:
        shapes = [jax.ShapeDtypeStruct((rows, width), jnp.bfloat16)]
    whole = pl.BlockSpec(memory_space=pltpu.VMEM)
    return pl.pallas_call(
        functools.partial(gram_body, apart),
        in_specs=[pl.BlockSpec(memory_space=pltpu.SMEM)] + [whole] * (len(pieces) + len(cols)),
        out_specs=[whole] * len(shapes),
        out_shape=shapes,
        scratch_shapes=[
            pltpu.VMEM((rows, len(cols) * obs), jnp.bfloat16),
            pltpu.VMEM((len(cols) * obs, width), jnp.bfloat16),
            pltpu.VMEM((rows, width), jnp.float32),
        ],
        compiler_params=pltpu.CompilerParams(vmem_limit_bytes=GRANT),
        name="gram",
    )(place, *pieces, *cols)


def on_device(pulses, wind_x, wind_y, obs_tile, obs_weight, obs_precision):
    tracers = pulses.shape[0]
    cells = lax.axis_size(CELLS)
    obs = obs_tile.shape[0]
    half = tracers // 2
    pulses = pulses.reshape(tracers * 4, 128)

    pulses = pltpu.with_memory_space_constraint(pulses, pltpu.HBM)
    messages = edges(pulses, wind_x, wind_y)
    halos = []
    for k in range(2):
        halos.append((shifted(messages[2 * k + 1], CELLS, 1), shifted(messages[2 * k], CELLS, -1)))
    sampled = None
    for span, (above, below) in zip(spans(tracers), halos):
        sampled = transport(pulses, above, below, wind_x, wind_y, span, sampled)

    tile = obs_tile[:, 0]
    order = jnp.arange(obs)
    earlier = (tile[:, None] == tile[None, :]) & (order[None, :] < order[:, None])
    slot = 2 * CAP * tile + jnp.sum(earlier.astype(jnp.int32), axis=1)
    lanes = jnp.arange(2 * CAP * cells)[None, :]
    chosen = [(slot[:, None] + CAP * h == lanes).astype(jnp.bfloat16) for h in range(2)]
    wide = obs_weight.astype(jnp.float32)
    averaging = (wide / jnp.sum(wide, axis=1, keepdims=True)).astype(jnp.bfloat16)
    split = obs_weight.shape[1] // 2
    rows_out = lax.dot_general(
        jnp.concatenate(chosen, axis=0),
        jnp.concatenate([averaging[:, :split], averaging[:, split:]], axis=0),
        (((0,), (0,)), ((), ())),
        preferred_element_type=jnp.float32,
    ).astype(jnp.bfloat16)
    rows_in = exchanged(rows_out.reshape(cells, 2 * CAP, split), CELLS)

    jac_tile = jacobian(rows_in.reshape(cells * 2 * CAP, split), sampled)
    group = lax.axis_size(XY)
    peers = lax.axis_size(TRACERS)
    deep = lax.axis_size("y")
    here = lax.axis_index(XY)
    odd = here % 2
    xl, y = lax.axis_index("xl"), lax.axis_index("y")
    owners = [here, (1 - xl) * deep + y]
    owners += [xl * deep + (y - d) % deep for d in range(1, deep)]
    owners += [(1 - xl) * deep + (y - d) % deep for d in range(1, deep)]
    tracer = lax.axis_index(TRACERS)
    row_owners = [2 * (tracer ^ flip) + (odd ^ s) for flip in (0, 2, 1, 3) for s in (0, 1)]
    place = jnp.stack(row_owners + owners + [lax.axis_index("z")]).astype(jnp.int32)
    precision = obs_precision.astype(jnp.float32)[:, None]
    even = odd == 0
    jac_tile, precision, place, even = lax.optimization_barrier((jac_tile, precision, place, even))
    jac_back = exchanged(jac_tile.reshape(cells, 2 * CAP, half), CELLS)
    jac_back = jac_back.reshape(cells * 2 * CAP, half)
    jac = [
        lax.dot_general(
            c, jac_back, (((1,), (0,)), ((), ())), preferred_element_type=jnp.float32
        )
        for c in chosen
    ]
    weighted = jnp.concatenate([(precision * j).astype(jnp.bfloat16) for j in jac], axis=1)
    cut = tracers * 5 // 8
    weighted = [weighted[:, :cut], weighted[:, cut:]]
    low, high = [j.astype(jnp.bfloat16) for j in jac]

    pairs = [(i // peers, i % peers) for i in range(group * peers)]
    to_same = [(a * peers + q, (2 * q + a % 2) * peers + a // 2) for a, q in pairs]
    to_cross = [(a * peers + q, (2 * q + 1 - a % 2) * peers + a // 2) for a, q in pairs]
    same = lax.ppermute(jnp.where(even, low, high), PLANE, to_same)
    cross = lax.ppermute(jnp.where(even, high, low), PLANE, to_cross)
    own = jnp.concatenate([same, cross], axis=0)
    across = shifted(own, "xh", 1)
    other = [shifted(own, "core", 1)]
    other.append(shifted(across, "core", 1))

    cols = []
    for part, value in enumerate(weighted):
        beside = shifted(value, "xl", 1)
        cols.append([value, beside])
        for source in (value, beside):
            for d in range(1, deep):
                cols[part].append(shifted(source, "y", d))

    depth = lax.axis_size("z")
    tile = gram_tile(place, [own, across, *other], cols[0], 0)[0]
    parts = exchanged(tile.reshape(depth, half // depth, cut), "z")
    total = jnp.sum(parts.astype(jnp.float32), axis=0)
    blocks = gram_tile(place, [own, across, *other], cols[1], depth)
    last = blocks[0]
    for d in (4, 3, 5, 2, 6, 1, 7):
        last = last + shifted(blocks[d], "z", d).astype(jnp.float32)
    return jnp.concatenate([total, last], axis=1)


def solution(mesh):
    fine = Mesh(mesh.devices.reshape(2, 4, 8, 2, 2), CELLS + TRACERS)
    placed = (
        P(TRACERS, CELLS, None),
        P(CELLS, None),
        P(CELLS, None),
        P(CELLS, None),
        P(CELLS, None),
        P(CELLS),
    )
    return jax.shard_map(
        on_device, mesh=fine, in_specs=placed, out_specs=P(CELLS, TRACERS), check_vma=False
    )
```

```python
import functools

import jax
import jax.numpy as jnp
from jax import lax
from jax.experimental import pallas as pl
from jax.experimental.pallas import tpu as pltpu
from jax.sharding import Mesh, PartitionSpec as P


STEPS = 3
CHUNKS = 4
GRANT = 16 * 1024 * 1024
CAP = 4
XY = ("xl", "y")
CELLS = ("xl", "y", "z")
TRACERS = ("xh", "core")
PLANE = XY + TRACERS


def shifted(value, axis, steps):
    count = lax.axis_size(axis)
    return lax.ppermute(value, axis, [(i, (i + steps) % count) for i in range(count)])


def exchanged(value, axis):
    return lax.all_to_all(value, axis, split_axis=0, concat_axis=0, tiled=True)


def edge_rows(pulse_ref, wind_x_ref, wind_y_ref, *refs):
    out_refs, (fetched_ref, winds_ref, sems) = refs[:-3], refs[-3:]
    tracers = pulse_ref.shape[0] // 4
    size = tracers // CHUNKS
    copies = []
    for k in range(CHUNKS):
        part = pl.ds(4 * k * size, 4 * size)
        copies.append(
            pltpu.make_async_copy(pulse_ref.at[part], fetched_ref.at[part], sems.at[k])
        )
    for k, ref in enumerate((wind_x_ref, wind_y_ref)):
        copies.append(pltpu.make_async_copy(ref, winds_ref.at[k], sems.at[CHUNKS + k]))
    for copy in copies:
        copy.start()
    for k in range(CHUNKS):
        copies[k].wait()
        rows = [
            fetched_ref[pl.ds(4 * k * size + r, size, 4), :].astype(jnp.bfloat16) for r in range(4)
        ]
        for part, (start, length) in enumerate(spans(tracers)):
            at = k * size - start
            if 0 <= at < length:
                for edge in range(2):
                    for r in range(STEPS):
                        out_refs[2 * part + edge][r * length + at : r * length + at + size] = rows[
                            r + edge
                        ]
    copies[CHUNKS].wait()
    copies[CHUNKS + 1].wait()
    winds = jnp.concatenate([winds_ref[0], winds_ref[1]], axis=0)
    coarse = winds.astype(jnp.bfloat16).astype(jnp.float32)
    both = jnp.concatenate([coarse, winds - coarse], axis=0).astype(jnp.bfloat16)
    for ref in out_refs:
        ref[ref.shape[0] - 16 :] = both


def spans(tracers):
    cut = tracers * 3 // 4
    return [(0, cut), (cut, tracers - cut)]


def edges(pulses, wind_x, wind_y):
    tracers = pulses.shape[0] // 4
    shapes = []
    for start, size in spans(tracers):
        shapes += [jax.ShapeDtypeStruct((STEPS * size + 16, 128), jnp.bfloat16)] * 2
    winds = [pltpu.with_memory_space_constraint(w, pltpu.HBM) for w in (wind_x, wind_y)]
    return pl.pallas_call(
        edge_rows,
        in_specs=[pl.BlockSpec(memory_space=pltpu.HBM)] * 3,
        out_specs=[pl.BlockSpec(memory_space=pltpu.VMEM)] * len(shapes),
        out_shape=shapes,
        scratch_shapes=[
            pltpu.VMEM(pulses.shape, jnp.float32),
            pltpu.VMEM((2, *wind_x.shape), jnp.float32),
            pltpu.SemaphoreType.DMA((CHUNKS + 2,)),
        ],
        compiler_params=pltpu.CompilerParams(vmem_limit_bytes=GRANT),
        name="edges",
    )(pulses, *winds)


PIECE = 64


def transport_body(
    pulse_ref, a0, a1, a2, b0, b1, b2, a_winds, b_winds, wind_x_ref, wind_y_ref, *refs
):
    out_ref, coef_ref = refs[-2:]
    count = out_ref.shape[0]

    @pl.when(pl.program_id(0) == 0)
    def _():
        above = a_winds[...].astype(jnp.float32)
        below = b_winds[...].astype(jnp.float32)
        above = above[0:8] + above[8:16]
        below = below[0:8] + below[8:16]
        wind_x = jnp.concatenate([above[2:4], wind_x_ref[...], below[0:2]], axis=0)
        wind_y = jnp.concatenate([above[6:8], wind_y_ref[...], below[4:6]], axis=0)
        next_y = jnp.concatenate([above[7:8], wind_y_ref[...], below[4:7]], axis=0)
        gain_x, loss_x = jnp.maximum(wind_x, 0.0), jnp.minimum(wind_x, 0.0)
        gain_y, loss_y = jnp.maximum(wind_y, 0.0), jnp.minimum(wind_y, 0.0)
        keep = 1.0 + loss_x - pltpu.roll(gain_x, 127, 1) + loss_y - jnp.maximum(next_y, 0.0)
        parts = [
            keep, gain_x, -pltpu.roll(loss_x, 127, 1), gain_y, -jnp.minimum(next_y, 0.0)
        ]
        for k, part in enumerate(parts):
            for w in range(8):
                coef_ref[k * 8 + w] = jnp.broadcast_to(part[w : w + 1], (PIECE, 128))

    for piece in range(count // PIECE):
        at = piece * PIECE
        field = (
            [ref[at : at + PIECE].astype(jnp.float32) for ref in (a0, a1, a2)]
            + [pulse_ref[pl.ds(4 * at + r, PIECE, 4), :] for r in range(4)]
            + [ref[at : at + PIECE].astype(jnp.float32) for ref in (b0, b1, b2)]
        )
        for step in range(STEPS):
            new = []
            for i in range(len(field) - 2):
                w = step + i
                here = field[i + 1]
                new.append(
                    coef_ref[w] * here
                    + coef_ref[8 + w] * pltpu.roll(here, 1, 1)
                    + coef_ref[16 + w] * pltpu.roll(here, 127, 1)
                    + coef_ref[24 + w] * field[i]
                    + coef_ref[32 + w] * field[i + 2]
                )
            field = new
        for r in range(4):
            out_ref[at : at + PIECE, r * 128 : (r + 1) * 128] = field[r].astype(jnp.bfloat16)


def transport(pulses, above, below, wind_x, wind_y, span, into=None, block=256):
    tracers = pulses.shape[0] // 4
    start, size = span
    skip, steps = start // block, size // block
    halo = [
        pl.BlockSpec((block, 128), lambda i, r=r: (r * steps + i, 0)) for r in range(STEPS)
    ]
    last = [pl.BlockSpec((16, 128), lambda i: (STEPS * size // 16, 0))] * 2
    wind = pl.BlockSpec((4, 128), lambda i: (0, 0))
    operands = [pulses, *[above] * 3, *[below] * 3, above, below, wind_x, wind_y]
    specs = [pl.BlockSpec((4 * block, 128), lambda i: (skip + i, 0))] + halo + halo + last
    specs += [wind, wind]
    aliases = {}
    if into is not None:
        aliases = {len(operands): 0}
        operands.append(into)
        specs.append(pl.BlockSpec(memory_space=pl.ANY))
    return pl.pallas_call(
        transport_body,
        grid=(steps,),
        in_specs=specs,
        out_specs=pl.BlockSpec((block, 512), lambda i: (skip + i, 0)),
        out_shape=jax.ShapeDtypeStruct((tracers, 512), jnp.bfloat16),
        scratch_shapes=[
            pltpu.VMEM((40, PIECE, 128), jnp.float32),
        ],
        input_output_aliases=aliases,
        compiler_params=pltpu.CompilerParams(vmem_limit_bytes=GRANT),
        name="transport",
    )(*operands)


def jacobian_body(rows_ref, low_ref, high_ref, out_ref, full_ref):
    @pl.when(pl.program_id(0) == 0)
    def _():
        count, width = rows_ref.shape
        mine = rows_ref[...].astype(jnp.float32).reshape(count // 8, 8, width)
        swap = pltpu.roll(mine, 4, 1)
        top = lax.broadcasted_iota(jnp.int32, mine.shape, 1) < 4
        left = jnp.where(top, mine, swap).reshape(count, width)
        right = jnp.where(top, swap, mine).reshape(count, width)
        full_ref[:, :width] = left.astype(jnp.bfloat16)
        full_ref[:, width:] = right.astype(jnp.bfloat16)

    dims = (((1,), (1,)), ((), ()))
    full = full_ref[...]
    low = lax.dot_general(full, low_ref[...], dims, preferred_element_type=jnp.float32)
    high = lax.dot_general(full, high_ref[...], dims, preferred_element_type=jnp.float32)
    row = lax.broadcasted_iota(jnp.int32, low.shape, 0)
    out_ref[...] = jnp.where((row & 4) == 0, low, high).astype(jnp.bfloat16)


def jacobian(rows, sampled, block=256):
    tracers = sampled.shape[0]
    count, width = rows.shape
    steps = tracers // 2 // block
    return pl.pallas_call(
        jacobian_body,
        grid=(steps,),
        in_specs=[
            pl.BlockSpec((count, width), lambda i: (0, 0)),
            pl.BlockSpec((block, 512), lambda i: (i, 0)),
            pl.BlockSpec((block, 512), lambda i: (steps + i, 0)),
        ],
        out_specs=pl.BlockSpec((count, block), lambda i: (0, i)),
        out_shape=jax.ShapeDtypeStruct((count, tracers // 2), jnp.bfloat16),
        scratch_shapes=[pltpu.VMEM((count, 2 * width), jnp.bfloat16)],
        compiler_params=pltpu.CompilerParams(vmem_limit_bytes=GRANT),
        name="jacobian",
    )(rows, sampled, sampled)


def gram_body(apart, place_ref, *refs):
    pieces, cols, outs, scratch = refs[:4], refs[4:12], refs[12:-3], refs[-3:]
    rows_ref, cols_ref, sum_ref = scratch
    block = cols[0].shape[0]
    parts = []
    for ref in pieces:
        parts += [ref[s : s + block] for s in range(0, ref.shape[0], block)]
    for k, part in enumerate(parts):
        at = pl.multiple_of(place_ref[k] * block, block)
        rows_ref[:, pl.ds(at, block)] = part.T
    for k, ref in enumerate(cols):
        at = pl.multiple_of(place_ref[8 + k] * block, block)
        cols_ref[pl.ds(at, block), :] = ref[...]
    tile = lax.dot_general(
        rows_ref[...], cols_ref[...], (((1,), (0,)), ((), ())), preferred_element_type=jnp.float32
    )
    if not apart:
        outs[0][...] = tile.astype(jnp.bfloat16)
        return
    sum_ref[...] = tile
    deep = len(outs)
    size = tile.shape[0] // deep
    for d, out_ref in enumerate(outs):
        at = pl.multiple_of(((place_ref[16] + d) % deep) * size, size)
        out_ref[...] = sum_ref[pl.ds(at, size), :].astype(out_ref.dtype)


def gram_tile(place, pieces, cols, apart):
    obs, width = cols[0].shape
    rows = pieces[0].shape[1]
    if apart:
        size = (rows // apart, width)
        shapes = [jax.ShapeDtypeStruct(size, jnp.float32)]
        shapes += [jax.ShapeDtypeStruct(size, jnp.bfloat16)] * (apart - 1)
    else:
        shapes = [jax.ShapeDtypeStruct((rows, width), jnp.bfloat16)]
    whole = pl.BlockSpec(memory_space=pltpu.VMEM)
    return pl.pallas_call(
        functools.partial(gram_body, apart),
        in_specs=[pl.BlockSpec(memory_space=pltpu.SMEM)] + [whole] * (len(pieces) + len(cols)),
        out_specs=[whole] * len(shapes),
        out_shape=shapes,
        scratch_shapes=[
            pltpu.VMEM((rows, len(cols) * obs), jnp.bfloat16),
            pltpu.VMEM((len(cols) * obs, width), jnp.bfloat16),
            pltpu.VMEM((rows, width), jnp.float32),
        ],
        compiler_params=pltpu.CompilerParams(vmem_limit_bytes=GRANT),
        name="gram",
    )(place, *pieces, *cols)


def on_device(pulses, wind_x, wind_y, obs_tile, obs_weight, obs_precision):
    tracers = pulses.shape[0]
    cells = lax.axis_size(CELLS)
    obs = obs_tile.shape[0]
    half = tracers // 2
    pulses = pulses.reshape(tracers * 4, 128)

    pulses = pltpu.with_memory_space_constraint(pulses, pltpu.HBM)
    messages = edges(pulses, wind_x, wind_y)
    halos = []
    for k in range(2):
        halos.append((shifted(messages[2 * k + 1], CELLS, 1), shifted(messages[2 * k], CELLS, -1)))
    sampled = None
    for span, (above, below) in zip(spans(tracers), halos):
        sampled = transport(pulses, above, below, wind_x, wind_y, span, sampled)

    tile = obs_tile[:, 0]
    order = jnp.arange(obs)
    earlier = (tile[:, None] == tile[None, :]) & (order[None, :] < order[:, None])
    slot = 2 * CAP * tile + jnp.sum(earlier.astype(jnp.int32), axis=1)
    lanes = jnp.arange(2 * CAP * cells)[None, :]
    chosen = [(slot[:, None] + CAP * h == lanes).astype(jnp.bfloat16) for h in range(2)]
    wide = obs_weight.astype(jnp.float32)
    averaging = (wide / jnp.sum(wide, axis=1, keepdims=True)).astype(jnp.bfloat16)
    split = obs_weight.shape[1] // 2
    rows_out = lax.dot_general(
        jnp.concatenate(chosen, axis=0),
        jnp.concatenate([averaging[:, :split], averaging[:, split:]], axis=0),
        (((0,), (0,)), ((), ())),
        preferred_element_type=jnp.float32,
    ).astype(jnp.bfloat16)
    rows_in = exchanged(rows_out.reshape(cells, 2 * CAP, split), CELLS)

    jac_tile = jacobian(rows_in.reshape(cells * 2 * CAP, split), sampled)
    group = lax.axis_size(XY)
    peers = lax.axis_size(TRACERS)
    deep = lax.axis_size("y")
    here = lax.axis_index(XY)
    odd = here % 2
    xl, y = lax.axis_index("xl"), lax.axis_index("y")
    owners = [here, (1 - xl) * deep + y]
    owners += [xl * deep + (y - d) % deep for d in range(1, deep)]
    owners += [(1 - xl) * deep + (y - d) % deep for d in range(1, deep)]
    tracer = lax.axis_index(TRACERS)
    row_owners = [2 * (tracer ^ flip) + (odd ^ s) for flip in (0, 2, 1, 3) for s in (0, 1)]
    place = jnp.stack(row_owners + owners + [lax.axis_index("z")]).astype(jnp.int32)
    precision = obs_precision.astype(jnp.float32)[:, None]
    even = odd == 0
    jac_tile, precision, place, even = lax.optimization_barrier((jac_tile, precision, place, even))
    jac_back = exchanged(jac_tile.reshape(cells, 2 * CAP, half), CELLS)
    jac_back = jac_back.reshape(cells * 2 * CAP, half)
    jac = [
        lax.dot_general(
            c, jac_back, (((1,), (0,)), ((), ())), preferred_element_type=jnp.float32
        )
        for c in chosen
    ]
    weighted = [(precision * j).astype(jnp.bfloat16) for j in jac]
    low, high = [j.astype(jnp.bfloat16) for j in jac]

    pairs = [(i // peers, i % peers) for i in range(group * peers)]
    to_same = [(a * peers + q, (2 * q + a % 2) * peers + a // 2) for a, q in pairs]
    to_cross = [(a * peers + q, (2 * q + 1 - a % 2) * peers + a // 2) for a, q in pairs]
    same = lax.ppermute(jnp.where(even, low, high), PLANE, to_same)
    cross = lax.ppermute(jnp.where(even, high, low), PLANE, to_cross)
    own = jnp.concatenate([same, cross], axis=0)
    across = shifted(own, "xh", 1)
    other = [shifted(own, "core", 1)]
    other.append(shifted(across, "core", 1))

    cols = []
    for part, value in enumerate(weighted):
        beside = shifted(value, "xl", 1)
        cols.append([value, beside])
        for source in (value, beside):
            for d in range(1, deep):
                cols[part].append(shifted(source, "y", d))

    depth = lax.axis_size("z")
    tile = gram_tile(place, [own, across, *other], cols[0], 0)[0]
    parts = exchanged(tile.reshape(depth, half // depth, half), "z")
    total = jnp.sum(parts.astype(jnp.float32), axis=0)
    blocks = gram_tile(place, [own, across, *other], cols[1], depth)
    last = blocks[0]
    for d in (4, 3, 5, 2, 6, 1, 7):
        last = last + shifted(blocks[d], "z", d).astype(jnp.float32)
    return jnp.concatenate([total, last], axis=1)


def solution(mesh):
    fine = Mesh(mesh.devices.reshape(2, 4, 8, 2, 2), CELLS + TRACERS)
    placed = (
        P(TRACERS, CELLS, None),
        P(CELLS, None),
        P(CELLS, None),
        P(CELLS, None),
        P(CELLS, None),
        P(CELLS),
    )
    return jax.shard_map(
        on_device, mesh=fine, in_specs=placed, out_specs=P(CELLS, TRACERS), check_vma=False
    )
```
